1024 devices in a mesh: seq: 16 (over z), exp: 16 (over y, core), head: 4 (over x).
Axes of the slice: x: 4, y: 8, z: 16, core: 2. Of those that a mesh axis runs over, the one named last changes fastest.
Arguments:
- query: bfloat16 [16, 8192, 2048], P('exp', 'seq', 'head'), may hold values from -6 to 6
- keys: bfloat16 [16, 8192, 2048], P('exp', 'seq', 'head'), may hold values from -6 to 6
- values: bfloat16 [16, 8192, 2048], P('exp', 'seq', 'head'), may hold values from -24 to 24
- attn_gain: float32 [2048], P('head'), may hold values from 0.5 to 1.5
- w_out: bfloat16 [2048, 2048], P('head'), may hold values from -0.125 to 0.125
- tokens: bfloat16 [16, 8192, 2048], P('exp', ('seq', 'head')), may hold values from -24 to 24
- routes: int32 [16, 8192, 2], P('exp', ('seq', 'head')), may hold values from 0 to 63, all different within a row; in each aligned block of 128 rows (0 to 127, 128 to 255, ..., all dimensions but the last counted through in order) at most 6 rows name the same one
- gates: float32 [16, 8192, 2], P('exp', ('seq', 'head')), may hold values from 0.25 to 1
- moe_gain: float32 [2048], replicated, may hold values from 0.5 to 1.5
- w_gate: bfloat16 [64, 2048, 384], P(('exp', 'head')), may hold values from -0.125 to 0.125
- w_up: bfloat16 [64, 2048, 384], P(('exp', 'head')), may hold values from -0.125 to 0.125
- w_down: bfloat16 [64, 384, 2048], P(('exp', 'head')), may hold values from -0.3125 to 0.3125
Outputs:
- mixed: bfloat16 [16, 8192, 2048], P('exp', ('seq', 'head'))
The draws below stay inside these ranges and needn't reach their ends.
Inputs may be any that keep to these rules, and one draw needn't show every extreme that they name: `routes`: the 2 picks of a token are different experts. In each aligned block of 128 tokens (the rows of one device) no expert is picked more than 6 times, and some expert is picked exactly 6 times in some blocks.
All inputs are finite; a program needn't handle non-finite values.
Results may differ from the reference program's by a relative error of at most 0.0049.
Values may be sent and summed in bfloat16 or wider, within the bound.
No kernel may reach another device: no remote copies, remote signals or barrier semaphores. Data moves between devices by JAX's collectives and lax.ppermute only.
A program may use at most 64 MiB of HBM per device.

```python
import math
import jax
import jax.numpy as jnp
import numpy as np
from jax import lax

D = 2048
HEADS = 16
HEAD_DIM = 128
FFN_H = 384
TOPK = 2
BLOCK = 512
SEQS = 16
LENGTH = 8192
TOK_DEV = 128
EXPERTS = 64
CAP = 6


def scaled_field(key, row_count, col_count):
    key_base = jax.random.fold_in(key, 17)
    key_rows = jax.random.fold_in(key, 29)
    key_cols = jax.random.fold_in(key, 41)
    base_draw = jax.random.normal(key_base, (row_count, col_count), jnp.float32)
    row_scale = jnp.exp(jax.random.uniform(key_rows, (row_count, 1), jnp.float32, math.log(0.3), math.log(3.0)))
    col_scale = jnp.exp(jax.random.uniform(key_cols, (1, col_count), jnp.float32, math.log(0.3), math.log(3.0)))
    return jnp.clip(base_draw * row_scale * col_scale, -24.0, 24.0)


def draw_tokens(key, part):
    field = scaled_field(jax.random.fold_in(key, 101), SEQS * LENGTH, D)
    return field.reshape(SEQS, LENGTH, D).astype(jnp.bfloat16)


def draw_values(key, part):
    field = scaled_field(jax.random.fold_in(key, 202), SEQS * LENGTH, HEADS * HEAD_DIM)
    return field.reshape(SEQS, LENGTH, HEADS * HEAD_DIM).astype(jnp.bfloat16)


def steps_of(stream_key, shape, split, low, top_value):
    loudness = 1.0
    for dim, blocks in split:
        heights = jax.random.uniform(jax.random.fold_in(jax.random.fold_in(stream_key, 6), dim), (blocks,), jnp.float32, low / len(split), top_value / len(split))
        loudness = loudness * jnp.repeat(jnp.exp(heights), shape[dim] // blocks).reshape((-1,) + (1,) * (len(shape) - 1 - dim))
    return loudness


def shared_out(own_key, own, number, rows, amount, top, most, slope):
    ranking = jax.random.permutation(own_key, amount)
    packed, usual = load_shares(amount, rows * top, most, slope, True), load_shares(amount, rows * top, most, slope, False)
    places = jnp.arange(amount)

    def named(lengths, turn):
        used = int((lengths > 0).sum())
        fixed = max(1, used // 4)
        moved = fixed + (places - fixed + turn * (used - fixed)) % max(1, amount - fixed)
        return jnp.zeros((amount,), jnp.int32).at[ranking[jnp.where(places < fixed, places, moved)]].set(jnp.asarray(lengths, jnp.int32))

    lengths = jnp.where(number % 4 == 0, named(packed, number // 4), named(usual, number - number // 4 - 1))
    mixed = jax.random.permutation(jax.random.fold_in(own, 3), amount)
    giver, taker = mixed[0:amount // 2 * 2:2], mixed[1:amount // 2 * 2:2]
    room = jnp.minimum(lengths[giver] - 1, most - lengths[taker]) // 2
    room = jnp.where((giver == ranking[0]) | (taker == ranking[0]) | (lengths[taker] == 0), 0, jnp.maximum(room, 0))
    moved = jax.random.randint(jax.random.fold_in(own, 4), (amount // 2,), 0, 1 << 20) % (room + 1)
    lengths = lengths.at[giver].add(-moved).at[taker].add(moved)
    labels = jnp.searchsorted(jnp.cumsum(lengths), jnp.arange(rows * top), side="right").astype(jnp.int32)
    table = labels.reshape(top, rows).T
    table = table[jax.random.permutation(jax.random.fold_in(own, 1), rows)]
    turn = jax.random.randint(jax.random.fold_in(own, 2), (rows, 1), 0, top)
    return jnp.take_along_axis(table, (jnp.arange(top)[None, :] + turn) % top, axis=1)


def load_shares(amount, total, bound, lean, full):
    weights = [(1 << 20) // math.isqrt(rank ** lean) + 1 for rank in range(1, amount + 1)]
    largest = bound if full else min(bound, max(-(-total // amount), total * weights[0] // sum(weights)))
    least = 1 if total - largest >= amount - 1 else 0
    given, spare = [largest] + [least] * (amount - 1), total - largest - least * (amount - 1)
    while spare > 0:
        candidates = [i for i in range(1, amount) if given[i] < largest] or [i for i in range(1, amount) if given[i] < bound]
        whole, remaining = sum([weights[i] for i in candidates]), spare
        for i in candidates:
            more = min(bound - given[i], max(1, remaining * weights[i] // whole), spare)
            given[i] = given[i] + more
            spare = spare - more
    return np.array(given)


def noise(own_key, dims, spread, most, cuts=(), held_as=jnp.bfloat16):
    array = spread * jax.random.normal(own_key, dims, jnp.float32)
    if cuts:
        array = array * steps_of(own_key, dims, cuts, -0.22, 0.18)
    return jnp.clip(array, -most, most).astype(held_as)


def setup_inputs(seed: int = 0) -> dict:
    streams_of = jax.random.split(jax.random.key(seed), 13)
    query = noise(streams_of[0], (SEQS, LENGTH, HEADS * HEAD_DIM), 1.0, 6.0, ((0, 16), (1, 16), (2, 4)))
    keys = noise(streams_of[1], (SEQS, LENGTH, HEADS * HEAD_DIM), 1.0, 6.0, ((0, 16), (1, 16), (2, 4)))
    values = draw_values(jax.random.fold_in(streams_of[12], 71), 0)
    attn_gain = jnp.clip(1.0 + 0.1 * jax.random.normal(streams_of[3], (HEADS * HEAD_DIM,), jnp.float32), 0.5, 1.5)
    w_out = noise(streams_of[4], (HEADS * HEAD_DIM, D), (HEADS * HEAD_DIM) ** -0.5, 0.125, ((0, 4),))
    tokens = draw_tokens(jax.random.fold_in(streams_of[12], 71), 0)
    routes_keys = jax.random.split(jax.random.fold_in(streams_of[6], 1), SEQS * LENGTH // TOK_DEV)
    routes_turns = jax.random.permutation(jax.random.fold_in(streams_of[6], 3), SEQS * LENGTH // TOK_DEV)
    routes = jax.vmap(lambda own, number: shared_out(jax.random.fold_in(streams_of[6], 2), own, number, TOK_DEV, EXPERTS, TOPK, CAP, 2))(routes_keys, routes_turns).reshape((SEQS, LENGTH, TOPK))
    gates = jnp.clip(0.25 + 0.75 * jax.random.uniform(streams_of[7], (SEQS, LENGTH, TOPK), jnp.float32) ** steps_of(streams_of[7], (SEQS, LENGTH, TOPK), ((0, 16), (1, 64)), -0.2, 0.2), 0.25, 1.0)
    moe_gain = jnp.clip(1.0 + 0.1 * jax.random.normal(streams_of[8], (D,), jnp.float32), 0.5, 1.5)
    w_gate = noise(streams_of[9], (EXPERTS, D, FFN_H), D ** -0.5, 0.125, ((0, 64),))
    w_up = noise(streams_of[10], (EXPERTS, D, FFN_H), D ** -0.5, 0.125, ((0, 64),))
    w_down = noise(streams_of[11], (EXPERTS, FFN_H, D), FFN_H ** -0.5, 0.3125, ((0, 64),))
    return dict(query=query, keys=keys, values=values, attn_gain=attn_gain, w_out=w_out, tokens=tokens, routes=routes, gates=gates, moe_gain=moe_gain, w_gate=w_gate, w_up=w_up, w_down=w_down)


EPSILON = 1e-06

def rms_scale(values_in, gain_vec):
    mean_square = lax.optimization_barrier(jnp.mean(values_in * values_in, axis=-1, keepdims=True))
    return values_in * lax.rsqrt(mean_square + EPSILON) * gain_vec

def attend(query_seq, keys_seq, values_seq, attn_gain):
    seq_rows = query_seq.shape[0]
    n_blocks = seq_rows // BLOCK
    block_shape = (n_blocks, BLOCK, HEADS, HEAD_DIM)
    query_blk = query_seq.reshape(block_shape)
    keys_blk = keys_seq.reshape(block_shape)
    values_blk = values_seq.reshape(block_shape)
    states = jnp.einsum('nbhd,nbhe->nhde', keys_blk.astype(jnp.float32), values_blk.astype(jnp.float32))
    running = jnp.cumsum(states, axis=0)
    prefix = jnp.concatenate([jnp.zeros_like(states[:1]), running[:-1]], axis=0).astype(jnp.bfloat16)
    causal = jnp.arange(BLOCK)[:, None] >= jnp.arange(BLOCK)[None, :]

    def one_block(pieces):
        query_one, keys_one, values_one, prefix_one = pieces
        scores = jnp.einsum('thd,shd->hts', query_one.astype(jnp.float32), keys_one.astype(jnp.float32))
        scores = jnp.where(causal[None, :, :], scores, jnp.zeros_like(scores)).astype(jnp.bfloat16)
        inner_sum = jnp.einsum('hts,she->the', scores.astype(jnp.float32), values_one.astype(jnp.float32))
        outer_sum = jnp.einsum('thd,hde->the', query_one.astype(jnp.float32), prefix_one.astype(jnp.float32))
        return inner_sum + outer_sum
    heads_out = lax.map(one_block, (query_blk, keys_blk, values_blk, prefix))
    normed = rms_scale(heads_out, attn_gain.reshape(HEADS, HEAD_DIM))
    return normed.astype(jnp.bfloat16).reshape(seq_rows, HEADS * HEAD_DIM)

def reference(query, keys, values, attn_gain, w_out, tokens, routes, gates, moe_gain, w_gate, w_up, w_down):

    def per_sequence(pieces):
        query_seq, keys_seq, values_seq, tokens_seq = pieces
        normed = attend(query_seq, keys_seq, values_seq, attn_gain)
        attn_out = jnp.dot(normed, w_out, preferred_element_type=jnp.float32)
        resid = tokens_seq.astype(jnp.float32) + attn_out
        moe_in = rms_scale(resid, moe_gain).astype(jnp.bfloat16)
        return (resid, moe_in)
    resid, moe_in = lax.map(per_sequence, (query, keys, values, tokens))
    flat_in = moe_in.reshape(-1, D)
    row_count = flat_in.shape[0]
    n_blocks = row_count // TOK_DEV
    picks = routes.reshape(n_blocks, TOK_DEV * TOPK)
    matches = (picks[:, :, None] == jnp.arange(EXPERTS, dtype=jnp.int32)[None, None, :]).astype(jnp.int32)
    earlier = jnp.cumsum(matches, axis=1) - matches
    position = lax.optimization_barrier(jnp.sum(earlier * matches, axis=2)).astype(jnp.int32)
    block_ids = jnp.arange(n_blocks, dtype=jnp.int32)[:, None]
    slot_index = ((block_ids * EXPERTS + picks) * CAP + position).reshape(-1).astype(jnp.int32)
    row_ids = (jnp.arange(row_count * TOPK, dtype=jnp.int32) // TOPK).astype(jnp.int32)
    slot_total = n_blocks * EXPERTS * CAP
    filler = jnp.full((slot_total,), row_count, jnp.int32).at[slot_index].set(row_ids)
    slot_gates = jnp.zeros((slot_total,), jnp.float32).at[slot_index].set(gates.reshape(-1))
    filler = filler.reshape(n_blocks, EXPERTS, CAP).transpose(1, 0, 2).reshape(EXPERTS, n_blocks * CAP)
    slot_gates = slot_gates.reshape(n_blocks, EXPERTS, CAP).transpose(1, 0, 2).reshape(EXPERTS, n_blocks * CAP)
    padded_in = jnp.concatenate([flat_in, jnp.zeros((1, D), jnp.bfloat16)], axis=0)

    def per_expert(moe_sum, pieces):
        rows_index, gate_values, gate_weight, up_weight, down_weight = pieces
        rows = padded_in[rows_index]
        gate_part = jnp.dot(rows, gate_weight, preferred_element_type=jnp.float32)
        up_part = jnp.dot(rows, up_weight, preferred_element_type=jnp.float32)
        hidden = (jax.nn.silu(gate_part) * up_part).astype(jnp.bfloat16)
        expert_out = jnp.dot(hidden, down_weight, preferred_element_type=jnp.float32).astype(jnp.bfloat16)
        moe_sum = moe_sum.at[rows_index].add(gate_values[:, None] * expert_out.astype(jnp.float32))
        return (moe_sum, None)
    moe_sum, _ = lax.scan(per_expert, jnp.zeros((row_count + 1, D), jnp.float32), (filler, slot_gates, w_gate, w_up, w_down))
    mixed = (resid.reshape(-1, D) + moe_sum[:row_count]).astype(jnp.bfloat16)
    return mixed.reshape(SEQS, LENGTH, D)
```

```python
import functools

import jax
import jax.numpy as jnp
from jax import lax
from jax.experimental import pallas as pl
from jax.experimental.pallas import tpu as pltpu
from jax.sharding import PartitionSpec as P

HEAD_DIM = 128
TOPK = 2
CAP = 6
QUARTERS = 4
GROUP = 8
EPSILON = 1e-06

BF16 = jnp.bfloat16
F32 = jnp.float32
I32 = jnp.int32


def vmem():
    return pl.BlockSpec(memory_space=pltpu.VMEM)


def dot(a, b, dims=((1,), (0,))):
    return lax.dot_general(a, b, (dims, ((), ())), preferred_element_type=F32)


def states_kernel(keys_ref, values_ref, out_ref):
    heads = keys_ref.shape[1] // HEAD_DIM
    for h in range(heads):
        cols = slice(h * HEAD_DIM, (h + 1) * HEAD_DIM)
        state = dot(keys_ref[:, cols], values_ref[:, cols], ((0,), (0,)))
        out_ref[cols, :] = state.astype(out_ref.dtype)


def scan_kernel(in_ref, out_ref):
    blocks = in_ref.shape[0]
    total = jnp.zeros(in_ref.shape[1:], F32)
    for b in range(blocks):
        out_ref[b] = total.astype(out_ref.dtype)
        total = total + in_ref[b].astype(F32)


def slots_kernel(routes_ref, cols_ref, rows_ref, *, experts):
    rows = routes_ref.shape[0]
    first, second = routes_ref[:, 0:1], routes_ref[:, 1:2]
    ids = lax.broadcasted_iota(I32, (rows, experts), 1)
    hit0 = (first == ids).astype(F32)
    hit1 = (second == ids).astype(F32)
    above = lax.broadcasted_iota(I32, (rows, rows), 0) > lax.broadcasted_iota(I32, (rows, rows), 1)
    before = dot(above.astype(F32).astype(BF16), (hit0 + hit1).astype(BF16))
    pos0 = jnp.sum(before * hit0, axis=1, keepdims=True)
    pos1 = jnp.sum(before * hit1, axis=1, keepdims=True)
    slot0 = first.astype(F32) * CAP + pos0
    slot1 = second.astype(F32) * CAP + pos1
    lane = lax.broadcasted_iota(I32, (rows, 128), 1)
    both = jnp.where(lane == 0, slot0, jnp.where(lane == 1, slot1, 0.0))
    cols_ref[...] = both.astype(I32)
    rows_ref[...] = both.T[0:8, :].astype(I32)


def attention_kernel(query_ref, keys_ref, values_ref, prefix_ref, gain_ref, w_ref, out_ref):
    i = pl.program_id(0)
    rows = query_ref.shape[0]
    length = keys_ref.shape[0]
    heads = query_ref.shape[1] // HEAD_DIM
    row_ids = lax.broadcasted_iota(I32, (rows, length), 0) + i * rows
    causal = row_ids >= lax.broadcasted_iota(I32, (rows, length), 1)
    parts = []
    for h in range(heads):
        cols = slice(h * HEAD_DIM, (h + 1) * HEAD_DIM)
        q = query_ref[:, cols]
        scores = dot(q, keys_ref[:, cols], ((1,), (1,)))
        scores = jnp.where(causal, scores, 0.0).astype(BF16)
        out = dot(scores, values_ref[:, cols]) + dot(q, prefix_ref[cols, :])
        scale = lax.rsqrt(jnp.mean(out * out, axis=-1, keepdims=True) + EPSILON)
        parts.append((out * scale * gain_ref[:, cols]).astype(BF16))
    normed = jnp.concatenate(parts, axis=1)
    out_ref[...] = dot(normed, w_ref[...]).astype(out_ref.dtype)


def row_keys(count, base):
    piece = QUARTERS * CAP
    r = lax.broadcasted_iota(I32, (count, 1), 0).astype(F32) + base
    e = jnp.floor((r + 0.5) * (1.0 / piece))
    rem = r - e * piece
    q = jnp.floor((rem + 0.5) * (1.0 / CAP))
    c = rem - q * CAP
    return (QUARTERS * (e * CAP + c) + q).astype(I32)


def dispatch_kernel(recv_ref, tokens_ref, gain_ref, rows_ref, resid_ref, out_ref):
    peers = recv_ref.shape[0]
    tok_rows, width = tokens_ref.shape
    attn = recv_ref[0].astype(F32)
    for p in range(1, peers):
        attn = attn + recv_ref[p].astype(F32)
    resid = tokens_ref[...].astype(F32) + attn
    resid_ref[...] = resid
    scale = lax.rsqrt(jnp.mean(resid * resid, axis=-1, keepdims=True) + EPSILON)
    moe_in = (resid * scale * gain_ref[...]).astype(BF16)
    part = width // QUARTERS
    stacked = jnp.concatenate([moe_in[:, q * part : (q + 1) * part] for q in range(QUARTERS)], axis=0)
    slots = rows_ref[...]
    key0 = jnp.concatenate([slots[0:1] * QUARTERS + q for q in range(QUARTERS)], axis=1)
    key1 = jnp.concatenate([slots[1:2] * QUARTERS + q for q in range(QUARTERS)], axis=1)
    total = out_ref.shape[0]
    chunk = total // 4
    for b in range(4):
        keys = row_keys(chunk, b * chunk)
        pick = ((keys == key0) | (keys == key1)).astype(F32).astype(BF16)
        out_ref[b * chunk : (b + 1) * chunk, :] = dot(pick, stacked).astype(BF16)


def regroup_matrix(to_pieces):
    n = GROUP * QUARTERS * CAP
    i = lax.broadcasted_iota(I32, (n, 1), 0).astype(F32)
    q = jnp.floor((i + 0.5) * (1.0 / (GROUP * CAP)))
    rem = i - q * (GROUP * CAP)
    p = jnp.floor((rem + 0.5) * (1.0 / CAP))
    c = rem - p * CAP
    source = (p * (QUARTERS * CAP) + q * CAP + c).astype(I32)
    j = lax.broadcasted_iota(I32, (n, n), 1)
    matrix = (source == j).astype(F32)
    if to_pieces:
        matrix = matrix.T
    return matrix.astype(BF16)


def expert_kernel(recv_ref, gate_ref, up_ref, down_ref, out_ref, x_ref):
    rows, part = recv_ref.shape
    n = GROUP * QUARTERS * CAP
    m = n // QUARTERS
    gather = regroup_matrix(False)
    for g in range(rows // n):
        block = dot(gather, recv_ref[g * n : (g + 1) * n, :]).astype(BF16)
        for q in range(QUARTERS):
            x_ref[g * m : (g + 1) * m, q * part : (q + 1) * part] = block[q * m : (q + 1) * m, :]
    x = x_ref[...]
    gate = dot(x, gate_ref[...])
    up = dot(x, up_ref[...])
    hidden = (gate / (1.0 + jnp.exp(-gate)) * up).astype(BF16)
    scatter = regroup_matrix(True)
    for g in range(rows // n):
        made = dot(hidden[g * m : (g + 1) * m, :], down_ref[...]).astype(BF16)
        block = jnp.concatenate([made[:, q * part : (q + 1) * part] for q in range(QUARTERS)], axis=0)
        out_ref[g * n : (g + 1) * n, :] = dot(scatter, block).astype(BF16)


def combine_kernel(back_ref, resid_ref, cols_ref, gates_ref, out_ref, y_ref):
    rows, part = back_ref.shape
    tok_rows = resid_ref.shape[0]
    n = GROUP * QUARTERS * CAP
    m = n // QUARTERS
    gather = regroup_matrix(False)
    for g in range(rows // n):
        block = dot(gather, back_ref[g * n : (g + 1) * n, :]).astype(BF16)
        for q in range(QUARTERS):
            y_ref[g * m : (g + 1) * m, q * part : (q + 1) * part] = block[q * m : (q + 1) * m, :]
    y = y_ref[...]
    slot_total = y.shape[0]
    ids = lax.broadcasted_iota(I32, (tok_rows, slot_total), 1)
    total = resid_ref[...]
    moe = jnp.zeros_like(total)
    for pick in range(TOPK):
        chosen = (cols_ref[:, pick : pick + 1] == ids).astype(F32).astype(BF16)
        moe = moe + gates_ref[:, pick : pick + 1] * dot(chosen, y)
    out_ref[...] = (total + moe).astype(out_ref.dtype)


def on_device(
    query, keys, values, attn_gain, w_out, tokens, routes, gates, moe_gain, w_gate, w_up, w_down
):
    query, keys, values = query[0], keys[0], values[0]
    tokens, routes, gates = tokens[0], routes[0], gates[0]
    w_gate, w_up, w_down = w_gate[0], w_up[0], w_down[0]
    length, feat = query.shape
    tok_rows, width = tokens.shape
    n_seq, n_exp, n_head = (lax.axis_size(a) for a in ("seq", "exp", "head"))
    experts = n_exp * n_head
    part = width // QUARTERS
    piece = QUARTERS * CAP

    states = pl.pallas_call(
        states_kernel,
        out_shape=jax.ShapeDtypeStruct((feat, HEAD_DIM), BF16),
        in_specs=[vmem(), vmem()],
        out_specs=vmem(),
        name="states",
    )(keys, values)
    spread = lax.all_to_all(states, "seq", split_axis=0, concat_axis=0, tiled=True)
    scanned = pl.pallas_call(
        scan_kernel,
        out_shape=jax.ShapeDtypeStruct((n_seq, feat // n_seq, HEAD_DIM), BF16),
        in_specs=[vmem()],
        out_specs=vmem(),
        name="scan",
    )(spread.reshape(n_seq, feat // n_seq, HEAD_DIM))
    prefix = lax.all_to_all(
        scanned.reshape(feat, HEAD_DIM), "seq", split_axis=0, concat_axis=0, tiled=True
    )

    slot_cols, slot_rows = pl.pallas_call(
        functools.partial(slots_kernel, experts=experts),
        out_shape=(
            jax.ShapeDtypeStruct((tok_rows, 128), I32),
            jax.ShapeDtypeStruct((8, tok_rows), I32),
        ),
        in_specs=[vmem()],
        out_specs=(vmem(), vmem()),
        name="slots",
    )(routes)

    partial_out = pl.pallas_call(
        attention_kernel,
        out_shape=jax.ShapeDtypeStruct((length, width), BF16),
        grid=(n_head,),
        in_specs=[
            pl.BlockSpec((length // n_head, feat), lambda i: (i, 0)),
            pl.BlockSpec((length, feat), lambda i: (0, 0)),
            pl.BlockSpec((length, feat), lambda i: (0, 0)),
            pl.BlockSpec((feat, HEAD_DIM), lambda i: (0, 0)),
            pl.BlockSpec((1, feat), lambda i: (0, 0)),
            pl.BlockSpec((feat, width), lambda i: (0, 0)),
        ],
        out_specs=pl.BlockSpec((length // n_head, width), lambda i: (i, 0)),
        name="attention",
    )(query, keys, values, prefix, attn_gain.reshape(1, feat), w_out)
    summed = lax.all_to_all(partial_out, "head", split_axis=0, concat_axis=0, tiled=True)

    resid, sent = pl.pallas_call(
        dispatch_kernel,
        out_shape=(
            jax.ShapeDtypeStruct((tok_rows, width), F32),
            jax.ShapeDtypeStruct((experts * piece, part), BF16),
        ),
        in_specs=[vmem()] * 4,
        out_specs=(vmem(), vmem()),
        name="dispatch",
    )(summed.reshape(n_head, tok_rows, width), tokens, moe_gain.reshape(1, width), slot_rows)
    received = lax.all_to_all(sent, ("exp", "head"), split_axis=0, concat_axis=0, tiled=True)
    made = pl.pallas_call(
        expert_kernel,
        out_shape=jax.ShapeDtypeStruct((experts * piece, part), BF16),
        in_specs=[vmem()] * 4,
        out_specs=vmem(),
        scratch_shapes=[pltpu.VMEM((experts * CAP, width), BF16)],
        name="experts",
    )(received, w_gate, w_up, w_down)
    returned = lax.all_to_all(made, ("exp", "head"), split_axis=0, concat_axis=0, tiled=True)
    mixed = pl.pallas_call(
        combine_kernel,
        out_shape=jax.ShapeDtypeStruct((tok_rows, width), BF16),
        in_specs=[vmem()] * 4,
        out_specs=vmem(),
        scratch_shapes=[pltpu.VMEM((experts * CAP, width), BF16)],
        name="combine",
    )(returned, resid, slot_cols, gates)
    return mixed[None]


def solution(mesh):
    in_specs = (
        P("exp", "seq", "head"),
        P("exp", "seq", "head"),
        P("exp", "seq", "head"),
        P("head"),
        P("head", None),
        P("exp", ("seq", "head"), None),
        P("exp", ("seq", "head"), None),
        P("exp", ("seq", "head"), None),
        P(),
        P(("exp", "head"), None, None),
        P(("exp", "head"), None, None),
        P(("exp", "head"), None, None),
    )
    out_specs = P("exp", ("seq", "head"), None)
    return jax.shard_map(
        on_device, mesh=mesh, in_specs=in_specs, out_specs=out_specs, check_vma=False
    )
```

```python
import functools
import math

import jax
import jax.numpy as jnp
from jax import lax
from jax.experimental import pallas as pl
from jax.experimental.pallas import tpu as pltpu
from jax.sharding import PartitionSpec as P

HEAD_DIM = 128
TOPK = 2
CAP = 6
QUARTERS = 4
GROUP = 8
EPSILON = 1e-06

BF16 = jnp.bfloat16
F32 = jnp.float32
I32 = jnp.int32


def vmem():
    return pl.BlockSpec(memory_space=pltpu.VMEM)


def call(kernel, args, out_shape, *, name, flops=10**6, limit=24, in_specs=None, **kwargs):
    outs = out_shape if isinstance(out_shape, tuple) else (out_shape,)
    if "out_specs" not in kwargs:
        kwargs["out_specs"] = tuple(vmem() for _ in outs) if isinstance(out_shape, tuple) else vmem()
    moved = sum(math.prod(a.shape) * jnp.dtype(a.dtype).itemsize for a in (*args, *outs))
    return pl.pallas_call(
        kernel,
        out_shape=out_shape,
        in_specs=in_specs or [vmem()] * len(args),
        cost_estimate=pl.CostEstimate(flops=flops, bytes_accessed=moved, transcendentals=0),
        compiler_params=pltpu.CompilerParams(vmem_limit_bytes=limit * 2**20),
        name=name,
        **kwargs,
    )(*args)


def dot(a, b, dims=((1,), (0,))):
    return lax.dot_general(a, b, (dims, ((), ())), preferred_element_type=F32)


def states_kernel(keys_ref, values_ref, out_ref):
    heads = keys_ref.shape[1] // HEAD_DIM
    for h in range(heads):
        cols = slice(h * HEAD_DIM, (h + 1) * HEAD_DIM)
        state = dot(keys_ref[:, cols], values_ref[:, cols], ((0,), (0,)))
        out_ref[cols, :] = state.astype(out_ref.dtype)


def scan_kernel(in_ref, out_ref):
    blocks = in_ref.shape[0]
    total = jnp.zeros(in_ref.shape[1:], F32)
    for b in range(blocks):
        out_ref[b] = total.astype(out_ref.dtype)
        total = total + in_ref[b].astype(F32)


def slots_kernel(routes_ref, cols_ref, pick_ref, *, experts):
    rows = routes_ref.shape[0]
    first, second = routes_ref[:, 0:1], routes_ref[:, 1:2]
    ids = lax.broadcasted_iota(I32, (rows, experts), 1)
    hit0 = (first == ids).astype(F32)
    hit1 = (second == ids).astype(F32)
    above = lax.broadcasted_iota(I32, (rows, rows), 0) > lax.broadcasted_iota(I32, (rows, rows), 1)
    before = dot(above.astype(F32).astype(BF16), (hit0 + hit1).astype(BF16))
    pos0 = jnp.sum(before * hit0, axis=1, keepdims=True)
    pos1 = jnp.sum(before * hit1, axis=1, keepdims=True)
    slot0 = first.astype(F32) * CAP + pos0
    slot1 = second.astype(F32) * CAP + pos1
    lane = lax.broadcasted_iota(I32, (rows, 128), 1)
    both = jnp.where(lane == 0, slot0, jnp.where(lane == 1, slot1, 0.0))
    cols_ref[...] = both.astype(I32)
    slots = both.T.astype(I32)
    key0 = jnp.concatenate([slots[0:1] * QUARTERS + q for q in range(QUARTERS)], axis=1)
    key1 = jnp.concatenate([slots[1:2] * QUARTERS + q for q in range(QUARTERS)], axis=1)
    total = pick_ref.shape[0]
    chunk = total // 4
    for b in range(4):
        keys = row_keys(chunk, b * chunk)
        pick = ((keys == key0) | (keys == key1)).astype(F32)
        pick_ref[b * chunk : (b + 1) * chunk, :] = pick.astype(BF16)


def inner_kernel(query_ref, keys_ref, values_ref, after_ref, out_ref):
    length = keys_ref.shape[0]
    heads = query_ref.shape[1] // HEAD_DIM
    rows = length // 4
    for i in range(4):
        seen = (i + 1) * rows
        row_ids = lax.broadcasted_iota(I32, (rows, seen), 0) + i * rows
        causal = row_ids >= lax.broadcasted_iota(I32, (rows, seen), 1)
        for h in range(heads):
            cols = slice(h * HEAD_DIM, (h + 1) * HEAD_DIM)
            q = query_ref[i * rows : (i + 1) * rows, cols]
            scores = dot(q, keys_ref[0:seen, cols], ((1,), (1,)))
            scores = jnp.where(causal, scores, 0.0).astype(BF16)
            out_ref[i * rows : (i + 1) * rows, cols] = dot(scores, values_ref[0:seen, cols])


def project_kernel(inner_ref, query_ref, prefix_ref, gain_ref, w_ref, out_ref, normed_ref, part_ref, sems):
    heads = query_ref.shape[1] // HEAD_DIM
    for h in range(heads):
        cols = slice(h * HEAD_DIM, (h + 1) * HEAD_DIM)
        out = inner_ref[:, cols] + dot(query_ref[:, cols], prefix_ref[cols, :])
        scale = lax.rsqrt(jnp.mean(out * out, axis=-1, keepdims=True) + EPSILON)
        normed_ref[:, cols] = (out * scale * gain_ref[:, cols]).astype(BF16)
    steps, _, _, part = part_ref.shape
    copies = []
    for j in range(steps):
        cols = slice(j * part, (j + 1) * part)
        part_ref[j] = dot(normed_ref[...], w_ref[:, cols]).astype(BF16).reshape(part_ref.shape[1:])
        copies.append(pltpu.make_async_copy(part_ref.at[j], out_ref.at[:, :, cols], sems.at[j]))
        copies[-1].start()
    for copy in copies:
        copy.wait()


def row_keys(count, base):
    piece = QUARTERS * CAP
    r = lax.broadcasted_iota(I32, (count, 1), 0).astype(F32) + base
    e = jnp.floor((r + 0.5) * (1.0 / piece))
    rem = r - e * piece
    q = jnp.floor((rem + 0.5) * (1.0 / CAP))
    c = rem - q * CAP
    return (QUARTERS * (e * CAP + c) + q).astype(I32)


def dispatch_kernel(recv_ref, tokens_ref, gain_ref, pick_ref, resid_ref, out_ref):
    peers = recv_ref.shape[0]
    width = tokens_ref.shape[1]
    attn = recv_ref[0].astype(F32)
    for p in range(1, peers):
        attn = attn + recv_ref[p].astype(F32)
    resid = tokens_ref[...].astype(F32) + attn
    resid_ref[...] = resid
    scale = lax.rsqrt(jnp.mean(resid * resid, axis=-1, keepdims=True) + EPSILON)
    moe_in = (resid * scale * gain_ref[...]).astype(BF16)
    part = width // QUARTERS
    stacked = jnp.concatenate([moe_in[:, q * part : (q + 1) * part] for q in range(QUARTERS)], axis=0)
    out_ref[...] = dot(pick_ref[...], stacked).astype(BF16)


def regroup_matrix(to_pieces):
    n = GROUP * QUARTERS * CAP
    i = lax.broadcasted_iota(I32, (n, 1), 0).astype(F32)
    q = jnp.floor((i + 0.5) * (1.0 / (GROUP * CAP)))
    rem = i - q * (GROUP * CAP)
    p = jnp.floor((rem + 0.5) * (1.0 / CAP))
    c = rem - p * CAP
    source = (p * (QUARTERS * CAP) + q * CAP + c).astype(I32)
    j = lax.broadcasted_iota(I32, (n, n), 1)
    matrix = (source == j).astype(F32)
    if to_pieces:
        matrix = matrix.T
    return matrix.astype(BF16)


def expert_kernel(recv_ref, gate_ref, up_ref, down_ref, out_ref, x_ref, y_ref, z_ref, sems):
    rows, part = recv_ref.shape
    n = GROUP * QUARTERS * CAP
    m = n // QUARTERS
    gather = regroup_matrix(False)
    for g in range(rows // n):
        block = dot(gather, recv_ref[g * n : (g + 1) * n, :]).astype(BF16)
        for q in range(QUARTERS):
            x_ref[g * m : (g + 1) * m, q * part : (q + 1) * part] = block[q * m : (q + 1) * m, :]
    x = x_ref[...]
    gate = dot(x, gate_ref[...])
    up = dot(x, up_ref[...])
    hidden = (gate / (1.0 + jnp.exp(-gate)) * up).astype(BF16)
    for q in range(QUARTERS):
        made = dot(hidden, down_ref[:, q * part : (q + 1) * part]).astype(BF16)
        for g in range(rows // n):
            y_ref[g * n + q * m : g * n + (q + 1) * m, :] = made[g * m : (g + 1) * m, :]
    scatter = regroup_matrix(True)
    copies = []
    for g in range(rows // n):
        part_rows = slice(g * n, (g + 1) * n)
        z_ref[part_rows, :] = dot(scatter, y_ref[part_rows, :]).astype(BF16)
        copies.append(pltpu.make_async_copy(z_ref.at[part_rows], out_ref.at[part_rows], sems.at[g]))
        copies[-1].start()
    for copy in copies:
        copy.wait()


def combine_kernel(back_ref, resid_ref, cols_ref, gates_ref, out_ref, y_ref):
    rows, part = back_ref.shape
    tok_rows = resid_ref.shape[0]
    n = GROUP * QUARTERS * CAP
    m = n // QUARTERS
    gather = regroup_matrix(False)
    for g in range(rows // n):
        block = dot(gather, back_ref[g * n : (g + 1) * n, :]).astype(BF16)
        for q in range(QUARTERS):
            y_ref[g * m : (g + 1) * m, q * part : (q + 1) * part] = block[q * m : (q + 1) * m, :]
    y = y_ref[...]
    slot_total = y.shape[0]
    ids = lax.broadcasted_iota(I32, (tok_rows, slot_total), 1)
    total = resid_ref[...]
    moe = jnp.zeros_like(total)
    for pick in range(TOPK):
        chosen = (cols_ref[:, pick : pick + 1] == ids).astype(F32).astype(BF16)
        moe = moe + gates_ref[:, pick : pick + 1] * dot(chosen, y)
    out_ref[...] = (total + moe).astype(out_ref.dtype)


def on_device(
    query, keys, values, attn_gain, w_out, tokens, routes, gates, moe_gain, w_gate, w_up, w_down
):
    query, keys, values = query[0], keys[0], values[0]
    tokens, routes, gates = tokens[0], routes[0], gates[0]
    w_gate, w_up, w_down = w_gate[0], w_up[0], w_down[0]
    length, feat = query.shape
    tok_rows, width = tokens.shape
    n_seq, n_exp, n_head = (lax.axis_size(a) for a in ("seq", "exp", "head"))
    experts = n_exp * n_head
    part = width // QUARTERS
    piece = QUARTERS * CAP

    states = call(
        states_kernel,
        (keys, values),
        jax.ShapeDtypeStruct((feat, HEAD_DIM), BF16),
        name="states",
        flops=2 * length * feat * HEAD_DIM,
    )
    spread = lax.all_to_all(states, "seq", split_axis=0, concat_axis=0, tiled=True)
    inner = call(
        inner_kernel,
        (query, keys, values, states),
        jax.ShapeDtypeStruct((length, feat), F32),
        in_specs=[vmem()] * 3 + [pl.BlockSpec(memory_space=pl.ANY)],
        name="inner",
        flops=4 * length * length * feat,
    )
    slot_cols, pick = call(
        functools.partial(slots_kernel, experts=experts),
        (routes,),
        (
            jax.ShapeDtypeStruct((tok_rows, 128), I32),
            jax.ShapeDtypeStruct((experts * piece, QUARTERS * tok_rows), BF16),
        ),
        name="slots",
        flops=10**8,
    )
    scanned = call(
        scan_kernel,
        (spread.reshape(n_seq, feat // n_seq, HEAD_DIM),),
        jax.ShapeDtypeStruct((n_seq, feat // n_seq, HEAD_DIM), BF16),
        name="scan",
    )
    prefix = lax.all_to_all(
        scanned.reshape(feat, HEAD_DIM), "seq", split_axis=0, concat_axis=0, tiled=True
    )
    partial_out = call(
        project_kernel,
        (inner, query, prefix, attn_gain.reshape(1, feat), w_out),
        pltpu.HBM((n_head, tok_rows, width), BF16),
        out_specs=pl.BlockSpec(memory_space=pltpu.HBM),
        scratch_shapes=[
            pltpu.VMEM((length, feat), BF16),
            pltpu.VMEM((QUARTERS, n_head, tok_rows, part), BF16),
            pltpu.SemaphoreType.DMA((QUARTERS,)),
        ],
        name="project",
        flops=2 * length * feat * width,
    )
    summed = lax.all_to_all(partial_out, "head", split_axis=0, concat_axis=0, tiled=False)

    resid, sent = call(
        dispatch_kernel,
        (summed.reshape(n_head, tok_rows, width), tokens, moe_gain.reshape(1, width), pick),
        (
            jax.ShapeDtypeStruct((tok_rows, width), F32),
            jax.ShapeDtypeStruct((experts * piece, part), BF16),
        ),
        name="dispatch",
        flops=2 * experts * piece * QUARTERS * tok_rows * part,
    )
    received = lax.all_to_all(sent, ("exp", "head"), split_axis=0, concat_axis=0, tiled=True)
    made = call(
        expert_kernel,
        (received, w_gate, w_up, w_down),
        jax.ShapeDtypeStruct((experts * piece, part), BF16),
        scratch_shapes=[
            pltpu.VMEM((experts * CAP, width), BF16),
            pltpu.VMEM((experts * piece, part), BF16),
            pltpu.VMEM((experts * piece, part), BF16),
            pltpu.SemaphoreType.DMA((experts // GROUP,)),
        ],
        out_specs=pl.BlockSpec(memory_space=pltpu.HBM),
        name="experts",
        flops=6 * experts * CAP * width * w_gate.shape[1],
    )
    returned = lax.all_to_all(made, ("exp", "head"), split_axis=0, concat_axis=0, tiled=True)
    mixed = call(
        combine_kernel,
        (returned, resid, slot_cols, gates),
        jax.ShapeDtypeStruct((tok_rows, width), BF16),
        scratch_shapes=[pltpu.VMEM((experts * CAP, width), BF16)],
        name="combine",
        flops=10**9,
    )
    return mixed[None]


def solution(mesh):
    in_specs = (
        P("exp", "seq", "head"),
        P("exp", "seq", "head"),
        P("exp", "seq", "head"),
        P("head"),
        P("head", None),
        P("exp", ("seq", "head"), None),
        P("exp", ("seq", "head"), None),
        P("exp", ("seq", "head"), None),
        P(),
        P(("exp", "head"), None, None),
        P(("exp", "head"), None, None),
        P(("exp", "head"), None, None),
    )
    out_specs = P("exp", ("seq", "head"), None)
    return jax.shard_map(
        on_device, mesh=mesh, in_specs=in_specs, out_specs=out_specs, check_vma=False
    )
```

```python
import functools
import math

import jax
import jax.numpy as jnp
from jax import lax
from jax.experimental import pallas as pl
from jax.experimental.pallas import tpu as pltpu
from jax.sharding import PartitionSpec as P

HEAD_DIM = 128
TOPK = 2
CAP = 6
QUARTERS = 4
GROUP = 8
EPSILON = 1e-06


BF16 = jnp.bfloat16
F32 = jnp.float32
I32 = jnp.int32


def vmem():
    return pl.BlockSpec(memory_space=pltpu.VMEM)


def call(kernel, args, out_shape, *, name, flops=10**6, limit=24, in_specs=None, **kwargs):
    outs = out_shape if isinstance(out_shape, tuple) else (out_shape,)
    if "out_specs" not in kwargs:
        kwargs["out_specs"] = tuple(vmem() for _ in outs) if isinstance(out_shape, tuple) else vmem()
    moved = sum(math.prod(a.shape) * jnp.dtype(a.dtype).itemsize for a in (*args, *outs))
    return pl.pallas_call(
        kernel,
        out_shape=out_shape,
        in_specs=in_specs or [vmem()] * len(args),
        cost_estimate=pl.CostEstimate(flops=flops, bytes_accessed=moved, transcendentals=0),
        compiler_params=pltpu.CompilerParams(vmem_limit_bytes=limit * 2**20),
        name=name,
        **kwargs,
    )(*args)


def anywhere():
    return pl.BlockSpec(memory_space=pl.ANY)


def dot(a, b, dims=((1,), (0,))):
    return lax.dot_general(a, b, (dims, ((), ())), preferred_element_type=F32)


def states_kernel(keys_hbm, values_hbm, out_ref, keys_ref, values_ref, sems):
    length, feat = keys_ref.shape
    chunks = sems.shape[1]
    rows = length // chunks
    copies = []
    for c in range(chunks):
        part = slice(c * rows, (c + 1) * rows)
        for k, (hbm, ref) in enumerate(((keys_hbm, keys_ref), (values_hbm, values_ref))):
            copies.append(pltpu.make_async_copy(hbm.at[part], ref.at[part], sems.at[k, c]))
            copies[-1].start()
    for copy in copies:
        copy.wait()
    for h in range(feat // HEAD_DIM):
        cols = slice(h * HEAD_DIM, (h + 1) * HEAD_DIM)
        state = dot(keys_ref[:, cols], values_ref[:, cols], ((0,), (0,)))
        out_ref[cols, :] = state.astype(out_ref.dtype)


def total_kernel(in_ref, out_ref):
    total = in_ref[0].astype(F32)
    for b in range(1, in_ref.shape[0]):
        total = total + in_ref[b].astype(F32)
    out_ref[...] = total.astype(out_ref.dtype)


def scan_kernel(in_ref, after_ref, *refs):
    *far_refs, out_ref = refs
    total = jnp.zeros(in_ref.shape[1:], F32)
    for far_ref in far_refs:
        total = total + far_ref[...].astype(F32)
    for b in range(in_ref.shape[0]):
        out_ref[b] = total.astype(out_ref.dtype)
        total = total + in_ref[b].astype(F32)


def slots_kernel(routes_ref, after_ref, cols_ref, pick_ref, *, experts):
    rows = routes_ref.shape[0]
    first, second = routes_ref[:, 0:1], routes_ref[:, 1:2]
    ids = lax.broadcasted_iota(I32, (rows, experts), 1)
    hit0 = (first == ids).astype(F32)
    hit1 = (second == ids).astype(F32)
    above = lax.broadcasted_iota(I32, (rows, rows), 0) > lax.broadcasted_iota(I32, (rows, rows), 1)
    before = dot(above.astype(F32).astype(BF16), (hit0 + hit1).astype(BF16))
    pos0 = jnp.sum(before * hit0, axis=1, keepdims=True)
    pos1 = jnp.sum(before * hit1, axis=1, keepdims=True)
    slot0 = first.astype(F32) * CAP + pos0
    slot1 = second.astype(F32) * CAP + pos1
    lane = lax.broadcasted_iota(I32, (rows, 128), 1)
    both = jnp.where(lane == 0, slot0, jnp.where(lane == 1, slot1, 0.0))
    cols_ref[...] = both.astype(I32)
    slots = both.T.astype(I32)
    key0 = jnp.concatenate([slots[0:1] * QUARTERS + q for q in range(QUARTERS)], axis=1)
    key1 = jnp.concatenate([slots[1:2] * QUARTERS + q for q in range(QUARTERS)], axis=1)
    total = pick_ref.shape[0]
    chunk = total // 4
    for b in range(4):
        keys = row_keys(chunk, b * chunk)
        pick = ((keys == key0) | (keys == key1)).astype(F32)
        pick_ref[b * chunk : (b + 1) * chunk, :] = pick.astype(BF16)


def inner_kernel(query_ref, keys_ref, values_ref, after_ref, out_ref):
    length = keys_ref.shape[0]
    heads = query_ref.shape[1] // HEAD_DIM
    rows = length // 4
    out_ref[:, query_ref.shape[1] :] = query_ref[...].astype(F32)
    for i in range(4):
        seen = (i + 1) * rows
        row_ids = lax.broadcasted_iota(I32, (rows, seen), 0) + i * rows
        causal = row_ids >= lax.broadcasted_iota(I32, (rows, seen), 1)
        for h in range(heads):
            cols = slice(h * HEAD_DIM, (h + 1) * HEAD_DIM)
            q = query_ref[i * rows : (i + 1) * rows, cols]
            scores = dot(q, keys_ref[0:seen, cols], ((1,), (1,)))
            scores = jnp.where(causal, scores, 0.0).astype(BF16)
            out_ref[i * rows : (i + 1) * rows, cols] = dot(scores, values_ref[0:seen, cols])


def project_kernel(inner_ref, prefix_ref, gain_ref, w_hbm, out_ref, w_ref, normed_ref, part_ref, w_sems, sems):
    steps, _, _, part = part_ref.shape
    loads = []
    for j in range(steps):
        cols = slice(j * part, (j + 1) * part)
        loads.append(pltpu.make_async_copy(w_hbm.at[:, cols], w_ref.at[:, cols], w_sems.at[j]))
        loads[-1].start()
    feat = normed_ref.shape[1]
    for h in range(feat // HEAD_DIM):
        cols = slice(h * HEAD_DIM, (h + 1) * HEAD_DIM)
        q = inner_ref[:, feat + h * HEAD_DIM : feat + (h + 1) * HEAD_DIM].astype(BF16)
        out = inner_ref[:, cols] + dot(q, prefix_ref[cols, :])
        scale = lax.rsqrt(jnp.mean(out * out, axis=-1, keepdims=True) + EPSILON)
        normed_ref[:, cols] = (out * scale * gain_ref[:, cols]).astype(BF16)
    copies = []
    for j in range(steps):
        cols = slice(j * part, (j + 1) * part)
        loads[j].wait()
        part_ref[j] = dot(normed_ref[...], w_ref[:, cols]).astype(BF16).reshape(part_ref.shape[1:])
        copies.append(pltpu.make_async_copy(part_ref.at[j], out_ref.at[:, :, cols], sems.at[j]))
        copies[-1].start()
    for copy in copies:
        copy.wait()


def row_keys(count, base):
    piece = QUARTERS * CAP
    r = lax.broadcasted_iota(I32, (count, 1), 0).astype(F32) + base
    e = jnp.floor((r + 0.5) * (1.0 / piece))
    rem = r - e * piece
    q = jnp.floor((rem + 0.5) * (1.0 / CAP))
    c = rem - q * CAP
    return (QUARTERS * (e * CAP + c) + q).astype(I32)


def dispatch_kernel(recv_ref, tokens_ref, gain_ref, pick_ref, resid_hbm, out_ref, resid_ref, sem):
    peers = recv_ref.shape[0]
    width = tokens_ref.shape[1]
    attn = recv_ref[0].astype(F32)
    for p in range(1, peers):
        attn = attn + recv_ref[p].astype(F32)
    resid = tokens_ref[...].astype(F32) + attn
    resid_ref[...] = resid
    copy = pltpu.make_async_copy(resid_ref, resid_hbm, sem)
    copy.start()
    scale = lax.rsqrt(jnp.mean(resid * resid, axis=-1, keepdims=True) + EPSILON)
    moe_in = (resid * scale * gain_ref[...]).astype(BF16)
    part = width // QUARTERS
    stacked = jnp.concatenate([moe_in[:, q * part : (q + 1) * part] for q in range(QUARTERS)], axis=0)
    out_ref[...] = dot(pick_ref[...], stacked).astype(BF16)
    copy.wait()


def regroup_matrix(to_pieces):
    n = GROUP * QUARTERS * CAP
    i = lax.broadcasted_iota(I32, (n, 1), 0).astype(F32)
    q = jnp.floor((i + 0.5) * (1.0 / (GROUP * CAP)))
    rem = i - q * (GROUP * CAP)
    p = jnp.floor((rem + 0.5) * (1.0 / CAP))
    c = rem - p * CAP
    source = (p * (QUARTERS * CAP) + q * CAP + c).astype(I32)
    j = lax.broadcasted_iota(I32, (n, n), 1)
    matrix = (source == j).astype(F32)
    if to_pieces:
        matrix = matrix.T
    return matrix.astype(BF16)


def expert_kernel(recv_ref, gate_ref, up_ref, down_ref, out_ref, x_ref, y_ref, z_ref, sems):
    rows, part = recv_ref.shape
    n = GROUP * QUARTERS * CAP
    m = n // QUARTERS
    gather = regroup_matrix(False)
    for g in range(rows // n):
        block = dot(gather, recv_ref[g * n : (g + 1) * n, :]).astype(BF16)
        for q in range(QUARTERS):
            x_ref[g * m : (g + 1) * m, q * part : (q + 1) * part] = block[q * m : (q + 1) * m, :]
    x = x_ref[...]
    gate = dot(x, gate_ref[...])
    up = dot(x, up_ref[...])
    hidden = (gate / (1.0 + jnp.exp(-gate)) * up).astype(BF16)
    for q in range(QUARTERS):
        made = dot(hidden, down_ref[:, q * part : (q + 1) * part]).astype(BF16)
        for g in range(rows // n):
            y_ref[g * n + q * m : g * n + (q + 1) * m, :] = made[g * m : (g + 1) * m, :]
    scatter = regroup_matrix(True)
    copies = []
    for g in range(rows // n):
        part_rows = slice(g * n, (g + 1) * n)
        z_ref[part_rows, :] = dot(scatter, y_ref[part_rows, :]).astype(BF16)
        copies.append(pltpu.make_async_copy(z_ref.at[part_rows], out_ref.at[part_rows], sems.at[g]))
        copies[-1].start()
    for copy in copies:
        copy.wait()


def combine_kernel(back_ref, resid_hbm, cols_ref, gates_ref, out_ref, y_ref, resid_ref, sem):
    rows, part = back_ref.shape
    tok_rows = resid_ref.shape[0]
    copy = pltpu.make_async_copy(resid_hbm, resid_ref, sem)
    copy.start()
    n = GROUP * QUARTERS * CAP
    m = n // QUARTERS
    gather = regroup_matrix(False)
    for g in range(rows // n):
        block = dot(gather, back_ref[g * n : (g + 1) * n, :]).astype(BF16)
        for q in range(QUARTERS):
            y_ref[g * m : (g + 1) * m, q * part : (q + 1) * part] = block[q * m : (q + 1) * m, :]
    y = y_ref[...]
    slot_total = y.shape[0]
    ids = lax.broadcasted_iota(I32, (tok_rows, slot_total), 1)
    moe = jnp.zeros(out_ref.shape, F32)
    for pick in range(TOPK):
        chosen = (cols_ref[:, pick : pick + 1] == ids).astype(F32).astype(BF16)
        moe = moe + gates_ref[:, pick : pick + 1] * dot(chosen, y)
    copy.wait()
    out_ref[...] = (resid_ref[...] + moe).astype(out_ref.dtype)


def on_device(
    query, keys, values, attn_gain, w_out, tokens, routes, gates, moe_gain, w_gate, w_up, w_down
):
    query, keys, values = query[0], keys[0], values[0]
    tokens, routes, gates = tokens[0], routes[0], gates[0]
    w_gate, w_up, w_down = w_gate[0], w_up[0], w_down[0]
    length, feat = query.shape
    tok_rows, width = tokens.shape
    n_seq, n_exp, n_head = (lax.axis_size(a) for a in ("seq", "exp", "head"))
    experts = n_exp * n_head
    part = width // QUARTERS
    piece = QUARTERS * CAP

    near = 4
    far = n_seq // near
    groups = [[near * g + i for i in range(near)] for g in range(far)]
    states = call(
        states_kernel,
        tuple(pltpu.with_memory_space_constraint(a, pltpu.HBM) for a in (keys, values)),
        jax.ShapeDtypeStruct((feat, HEAD_DIM), BF16),
        in_specs=[anywhere(), anywhere()],
        scratch_shapes=[
            pltpu.VMEM((length, feat), BF16),
            pltpu.VMEM((length, feat), BF16),
            pltpu.SemaphoreType.DMA((2, 4)),
        ],
        name="states",
        flops=2 * length * feat * HEAD_DIM,
        limit=8,
    )
    shared = lax.all_to_all(
        states, "seq", split_axis=0, concat_axis=0, tiled=True, axis_index_groups=groups
    ).reshape(near, feat // near, HEAD_DIM)
    slice_shape = (feat // near, HEAD_DIM)
    group_total = call(
        total_kernel, (shared,), jax.ShapeDtypeStruct(slice_shape, BF16), name="total", limit=4
    )
    slot_cols, pick = call(
        functools.partial(slots_kernel, experts=experts),
        (routes, group_total),
        (
            jax.ShapeDtypeStruct((tok_rows, 128), I32),
            jax.ShapeDtypeStruct((experts * piece, QUARTERS * tok_rows), BF16),
        ),
        in_specs=[vmem(), anywhere()],
        name="slots",
        flops=10**8,
        limit=12,
    )
    earlier = [
        lax.ppermute(group_total, "seq", [(i, i + near * k) for i in range(n_seq - near * k)])
        for k in range(1, far)
    ]
    scanned = call(
        scan_kernel,
        (shared, slot_cols, *earlier),
        jax.ShapeDtypeStruct((near, *slice_shape), BF16),
        in_specs=[vmem(), anywhere()] + [vmem()] * len(earlier),
        name="scan",
        limit=4,
    )
    prefix = lax.all_to_all(
        scanned.reshape(feat, HEAD_DIM),
        "seq",
        split_axis=0,
        concat_axis=0,
        tiled=True,
        axis_index_groups=groups,
    )
    inner = call(
        inner_kernel,
        (query, keys, values, states),
        jax.ShapeDtypeStruct((length, 2 * feat), F32),
        in_specs=[vmem()] * 3 + [anywhere()],
        name="inner",
        flops=4 * length * length * feat,
        limit=12,
    )
    partial_out = call(
        project_kernel,
        (inner, prefix, attn_gain.reshape(1, feat), pltpu.with_memory_space_constraint(w_out, pltpu.HBM)),
        pltpu.HBM((n_head, tok_rows, width), BF16),
        in_specs=[vmem()] * 3 + [pl.BlockSpec(memory_space=pltpu.HBM)],
        out_specs=pl.BlockSpec(memory_space=pltpu.HBM),
        scratch_shapes=[
            pltpu.VMEM((feat, width), BF16),
            pltpu.VMEM((length, feat), BF16),
            pltpu.VMEM((QUARTERS, n_head, tok_rows, part), BF16),
            pltpu.SemaphoreType.DMA((QUARTERS,)),
            pltpu.SemaphoreType.DMA((QUARTERS,)),
        ],
        name="project",
        limit=12,
        flops=2 * length * feat * width,
    )
    summed = lax.all_to_all(partial_out, "head", split_axis=0, concat_axis=0, tiled=False)

    resid, sent = call(
        dispatch_kernel,
        (summed.reshape(n_head, tok_rows, width), tokens, moe_gain.reshape(1, width), pick),
        (
            pltpu.HBM((tok_rows, width), F32),
            jax.ShapeDtypeStruct((experts * piece, part), BF16),
        ),
        out_specs=(pl.BlockSpec(memory_space=pltpu.HBM), vmem()),
        scratch_shapes=[pltpu.VMEM((tok_rows, width), F32), pltpu.SemaphoreType.DMA],
        name="dispatch",
        limit=16,
        flops=2 * experts * piece * QUARTERS * tok_rows * part,
    )
    received = lax.all_to_all(sent, ("exp", "head"), split_axis=0, concat_axis=0, tiled=True)
    made = call(
        expert_kernel,
        (received, w_gate, w_up, w_down),
        jax.ShapeDtypeStruct((experts * piece, part), BF16),
        scratch_shapes=[
            pltpu.VMEM((experts * CAP, width), BF16),
            pltpu.VMEM((experts * piece, part), BF16),
            pltpu.VMEM((experts * piece, part), BF16),
            pltpu.SemaphoreType.DMA((experts // GROUP,)),
        ],
        out_specs=pl.BlockSpec(memory_space=pltpu.HBM),
        name="experts",
        limit=20,
        flops=6 * experts * CAP * width * w_gate.shape[1],
    )
    returned = lax.all_to_all(made, ("exp", "head"), split_axis=0, concat_axis=0, tiled=True)
    mixed = call(
        combine_kernel,
        (returned, resid, slot_cols, gates),
        jax.ShapeDtypeStruct((tok_rows, width), BF16),
        in_specs=[vmem(), pl.BlockSpec(memory_space=pltpu.HBM), vmem(), vmem()],
        scratch_shapes=[
            pltpu.VMEM((experts * CAP, width), BF16),
            pltpu.VMEM((tok_rows, width), F32),
            pltpu.SemaphoreType.DMA,
        ],
        name="combine",
        limit=16,
        flops=10**9,
    )
    return mixed[None]


def solution(mesh):
    in_specs = (
        P("exp", "seq", "head"),
        P("exp", "seq", "head"),
        P("exp", "seq", "head"),
        P("head"),
        P("head", None),
        P("exp", ("seq", "head"), None),
        P("exp", ("seq", "head"), None),
        P("exp", ("seq", "head"), None),
        P(),
        P(("exp", "head"), None, None),
        P(("exp", "head"), None, None),
        P(("exp", "head"), None, None),
    )
    out_specs = P("exp", ("seq", "head"), None)
    return jax.shard_map(
        on_device, mesh=mesh, in_specs=in_specs, out_specs=out_specs, check_vma=False
    )
```

```python
import functools
import math

import jax
import jax.numpy as jnp
from jax import lax
from jax.experimental import pallas as pl
from jax.experimental.pallas import tpu as pltpu
from jax.sharding import PartitionSpec as P

HEAD_DIM = 128
TOPK = 2
CAP = 6
QUARTERS = 4
GROUP = 8
EPSILON = 1e-06


BF16 = jnp.bfloat16
F32 = jnp.float32
I32 = jnp.int32


def vmem():
    return pl.BlockSpec(memory_space=pltpu.VMEM)


def call(kernel, args, out_shape, *, name, flops=10**6, limit=24, in_specs=None, **kwargs):
    outs = out_shape if isinstance(out_shape, tuple) else (out_shape,)
    if "out_specs" not in kwargs:
        kwargs["out_specs"] = tuple(vmem() for _ in outs) if isinstance(out_shape, tuple) else vmem()
    moved = sum(math.prod(a.shape) * jnp.dtype(a.dtype).itemsize for a in (*args, *outs))
    return pl.pallas_call(
        kernel,
        out_shape=out_shape,
        in_specs=in_specs or [vmem()] * len(args),
        cost_estimate=pl.CostEstimate(flops=flops, bytes_accessed=moved, transcendentals=0),
        compiler_params=pltpu.CompilerParams(vmem_limit_bytes=limit * 2**20),
        name=name,
        **kwargs,
    )(*args)


def anywhere():
    return pl.BlockSpec(memory_space=pl.ANY)


def dot(a, b, dims=((1,), (0,))):
    return lax.dot_general(a, b, (dims, ((), ())), preferred_element_type=F32)


def states_kernel(keys_hbm, values_hbm, out_ref, keys_ref, values_ref, sems):
    length, feat = keys_ref.shape
    chunks = sems.shape[1]
    rows = length // chunks
    copies = []
    for c in range(chunks):
        part = slice(c * rows, (c + 1) * rows)
        for k, (hbm, ref) in enumerate(((keys_hbm, keys_ref), (values_hbm, values_ref))):
            copies.append(pltpu.make_async_copy(hbm.at[part], ref.at[part], sems.at[k, c]))
            copies[-1].start()
    for copy in copies:
        copy.wait()
    for h in range(feat // HEAD_DIM):
        cols = slice(h * HEAD_DIM, (h + 1) * HEAD_DIM)
        state = dot(keys_ref[:, cols], values_ref[:, cols], ((0,), (0,)))
        out_ref[cols, :] = state.astype(out_ref.dtype)


def total_kernel(in_ref, after_ref, out_ref):
    total = in_ref[0].astype(F32)
    for b in range(1, in_ref.shape[0]):
        total = total + in_ref[b].astype(F32)
    out_ref[...] = total.astype(out_ref.dtype)


def scan_kernel(in_ref, *refs):
    *far_refs, out_ref = refs
    total = jnp.zeros(in_ref.shape[1:], F32)
    for far_ref in far_refs:
        total = total + far_ref[...].astype(F32)
    for b in range(in_ref.shape[0]):
        out_ref[b] = total.astype(out_ref.dtype)
        total = total + in_ref[b].astype(F32)


def slots_kernel(routes_ref, after_ref, cols_ref, pick_ref, *, experts):
    rows = routes_ref.shape[0]
    first, second = routes_ref[:, 0:1], routes_ref[:, 1:2]
    ids = lax.broadcasted_iota(I32, (rows, experts), 1)
    hit0 = (first == ids).astype(F32)
    hit1 = (second == ids).astype(F32)
    above = lax.broadcasted_iota(I32, (rows, rows), 0) > lax.broadcasted_iota(I32, (rows, rows), 1)
    before = dot(above.astype(F32).astype(BF16), (hit0 + hit1).astype(BF16))
    pos0 = jnp.sum(before * hit0, axis=1, keepdims=True)
    pos1 = jnp.sum(before * hit1, axis=1, keepdims=True)
    slot0 = first.astype(F32) * CAP + pos0
    slot1 = second.astype(F32) * CAP + pos1
    lane = lax.broadcasted_iota(I32, (rows, 128), 1)
    both = jnp.where(lane == 0, slot0, jnp.where(lane == 1, slot1, 0.0))
    cols_ref[...] = both.astype(I32)
    slots = both.T.astype(I32)
    key0 = jnp.concatenate([slots[0:1] * QUARTERS + q for q in range(QUARTERS)], axis=1)
    key1 = jnp.concatenate([slots[1:2] * QUARTERS + q for q in range(QUARTERS)], axis=1)
    total = pick_ref.shape[0]
    chunk = total // 4
    for b in range(4):
        keys = row_keys(chunk, b * chunk)
        pick = ((keys == key0) | (keys == key1)).astype(F32)
        pick_ref[b * chunk : (b + 1) * chunk, :] = pick.astype(BF16)


def inner_kernel(query_ref, keys_ref, values_ref, after_ref, out_ref):
    length = keys_ref.shape[0]
    heads = query_ref.shape[1] // HEAD_DIM
    rows = length // 4
    out_ref[:, query_ref.shape[1] :] = query_ref[...].astype(F32)
    for i in range(4):
        seen = (i + 1) * rows
        row_ids = lax.broadcasted_iota(I32, (rows, seen), 0) + i * rows
        causal = row_ids >= lax.broadcasted_iota(I32, (rows, seen), 1)
        for h in range(heads):
            cols = slice(h * HEAD_DIM, (h + 1) * HEAD_DIM)
            q = query_ref[i * rows : (i + 1) * rows, cols]
            scores = dot(q, keys_ref[0:seen, cols], ((1,), (1,)))
            scores = jnp.where(causal, scores, 0.0).astype(BF16)
            out_ref[i * rows : (i + 1) * rows, cols] = dot(scores, values_ref[0:seen, cols])


def stage_kernel(w_hbm, after_ref, w_ref, sems):
    pieces = sems.shape[0]
    rows = w_ref.shape[0] // pieces
    loads = []
    for p in range(pieces):
        part = slice(p * rows, (p + 1) * rows)
        source = w_hbm.at[part, 0 : w_ref.shape[1]]
        loads.append(pltpu.make_async_copy(source, w_ref.at[part], sems.at[p]))
        loads[-1].start()
    for load in loads:
        load.wait()


def project_kernel(
    inner_ref, prefix_ref, gain_ref, w_near_ref, w_hbm, out_ref, w_ref, normed_ref, part_ref, w_sems, sems
):
    steps, _, _, part = part_ref.shape
    ready = w_near_ref.shape[1] // part
    loads = []
    for j in range(ready, steps):
        source = w_hbm.at[:, j * part : (j + 1) * part]
        loads.append(pltpu.make_async_copy(source, w_ref.at[j - ready], w_sems.at[j - ready]))
        loads[-1].start()
    feat = normed_ref.shape[1]
    for h in range(feat // HEAD_DIM):
        cols = slice(h * HEAD_DIM, (h + 1) * HEAD_DIM)
        q = inner_ref[:, feat + h * HEAD_DIM : feat + (h + 1) * HEAD_DIM].astype(BF16)
        out = inner_ref[:, cols] + dot(q, prefix_ref[cols, :])
        scale = lax.rsqrt(jnp.mean(out * out, axis=-1, keepdims=True) + EPSILON)
        normed_ref[:, cols] = (out * scale * gain_ref[:, cols]).astype(BF16)
    copies = []
    for j in range(steps):
        cols = slice(j * part, (j + 1) * part)
        if j < ready:
            w = w_near_ref[:, cols]
        else:
            loads[j - ready].wait()
            w = w_ref[j - ready]
        part_ref[j] = dot(normed_ref[...], w).astype(BF16).reshape(part_ref.shape[1:])
        copies.append(pltpu.make_async_copy(part_ref.at[j], out_ref.at[:, :, cols], sems.at[j]))
        copies[-1].start()
    for copy in copies:
        copy.wait()


def row_keys(count, base):
    piece = QUARTERS * CAP
    r = lax.broadcasted_iota(I32, (count, 1), 0).astype(F32) + base
    e = jnp.floor((r + 0.5) * (1.0 / piece))
    rem = r - e * piece
    q = jnp.floor((rem + 0.5) * (1.0 / CAP))
    c = rem - q * CAP
    return (QUARTERS * (e * CAP + c) + q).astype(I32)


def dispatch_kernel(recv_ref, tokens_ref, gain_ref, pick_ref, resid_hbm, out_ref, resid_ref, sem):
    peers = recv_ref.shape[0]
    width = tokens_ref.shape[1]
    attn = recv_ref[0].astype(F32)
    for p in range(1, peers):
        attn = attn + recv_ref[p].astype(F32)
    resid = tokens_ref[...].astype(F32) + attn
    resid_ref[...] = resid
    copy = pltpu.make_async_copy(resid_ref, resid_hbm, sem)
    copy.start()
    scale = lax.rsqrt(jnp.mean(resid * resid, axis=-1, keepdims=True) + EPSILON)
    moe_in = (resid * scale * gain_ref[...]).astype(BF16)
    part = width // QUARTERS
    stacked = jnp.concatenate([moe_in[:, q * part : (q + 1) * part] for q in range(QUARTERS)], axis=0)
    out_ref[...] = dot(pick_ref[...], stacked).astype(BF16)
    copy.wait()


def regroup_matrix(to_pieces):
    n = GROUP * QUARTERS * CAP
    i = lax.broadcasted_iota(I32, (n, 1), 0).astype(F32)
    q = jnp.floor((i + 0.5) * (1.0 / (GROUP * CAP)))
    rem = i - q * (GROUP * CAP)
    p = jnp.floor((rem + 0.5) * (1.0 / CAP))
    c = rem - p * CAP
    source = (p * (QUARTERS * CAP) + q * CAP + c).astype(I32)
    j = lax.broadcasted_iota(I32, (n, n), 1)
    matrix = (source == j).astype(F32)
    if to_pieces:
        matrix = matrix.T
    return matrix.astype(BF16)


def expert_kernel(recv_ref, gate_ref, up_ref, down_ref, out_ref, x_ref, y_ref, z_ref, sems):
    rows, part = recv_ref.shape
    n = GROUP * QUARTERS * CAP
    m = n // QUARTERS
    gather = regroup_matrix(False)
    for g in range(rows // n):
        block = dot(gather, recv_ref[g * n : (g + 1) * n, :]).astype(BF16)
        for q in range(QUARTERS):
            x_ref[g * m : (g + 1) * m, q * part : (q + 1) * part] = block[q * m : (q + 1) * m, :]
    x = x_ref[...]
    gate = dot(x, gate_ref[...])
    up = dot(x, up_ref[...])
    hidden = (gate / (1.0 + jnp.exp(-gate)) * up).astype(BF16)
    for q in range(QUARTERS):
        made = dot(hidden, down_ref[:, q * part : (q + 1) * part]).astype(BF16)
        for g in range(rows // n):
            y_ref[g * n + q * m : g * n + (q + 1) * m, :] = made[g * m : (g + 1) * m, :]
    scatter = regroup_matrix(True)
    copies = []
    for g in range(rows // n):
        part_rows = slice(g * n, (g + 1) * n)
        z_ref[part_rows, :] = dot(scatter, y_ref[part_rows, :]).astype(BF16)
        copies.append(pltpu.make_async_copy(z_ref.at[part_rows], out_ref.at[part_rows], sems.at[g]))
        copies[-1].start()
    for copy in copies:
        copy.wait()


def combine_kernel(back_ref, resid_hbm, cols_ref, gates_ref, out_ref, y_ref, resid_ref, sem):
    rows, part = back_ref.shape
    tok_rows = resid_ref.shape[0]
    copy = pltpu.make_async_copy(resid_hbm, resid_ref, sem)
    copy.start()
    n = GROUP * QUARTERS * CAP
    m = n // QUARTERS
    gather = regroup_matrix(False)
    for g in range(rows // n):
        block = dot(gather, back_ref[g * n : (g + 1) * n, :]).astype(BF16)
        for q in range(QUARTERS):
            y_ref[g * m : (g + 1) * m, q * part : (q + 1) * part] = block[q * m : (q + 1) * m, :]
    y = y_ref[...]
    slot_total = y.shape[0]
    ids = lax.broadcasted_iota(I32, (tok_rows, slot_total), 1)
    moe = jnp.zeros(out_ref.shape, F32)
    for pick in range(TOPK):
        chosen = (cols_ref[:, pick : pick + 1] == ids).astype(F32).astype(BF16)
        moe = moe + gates_ref[:, pick : pick + 1] * dot(chosen, y)
    copy.wait()
    out_ref[...] = (resid_ref[...] + moe).astype(out_ref.dtype)


def on_device(
    query, keys, values, attn_gain, w_out, tokens, routes, gates, moe_gain, w_gate, w_up, w_down
):
    query, keys, values = query[0], keys[0], values[0]
    tokens, routes, gates = tokens[0], routes[0], gates[0]
    w_gate, w_up, w_down = w_gate[0], w_up[0], w_down[0]
    length, feat = query.shape
    tok_rows, width = tokens.shape
    n_seq, n_exp, n_head = (lax.axis_size(a) for a in ("seq", "exp", "head"))
    experts = n_exp * n_head
    part = width // QUARTERS
    piece = QUARTERS * CAP

    near = 4
    far = n_seq // near
    groups = [[near * g + i for i in range(near)] for g in range(far)]
    states = call(
        states_kernel,
        tuple(pltpu.with_memory_space_constraint(a, pltpu.HBM) for a in (keys, values)),
        jax.ShapeDtypeStruct((feat, HEAD_DIM), BF16),
        in_specs=[anywhere(), anywhere()],
        scratch_shapes=[
            pltpu.VMEM((length, feat), BF16),
            pltpu.VMEM((length, feat), BF16),
            pltpu.SemaphoreType.DMA((2, 4)),
        ],
        name="states",
        flops=2 * length * feat * HEAD_DIM,
        limit=8,
    )
    shared = lax.all_to_all(
        states, "seq", split_axis=0, concat_axis=0, tiled=True, axis_index_groups=groups
    ).reshape(near, feat // near, HEAD_DIM)
    slice_shape = (feat // near, HEAD_DIM)
    slot_cols, pick = call(
        functools.partial(slots_kernel, experts=experts),
        (routes, states),
        (
            jax.ShapeDtypeStruct((tok_rows, 128), I32),
            jax.ShapeDtypeStruct((experts * piece, QUARTERS * tok_rows), BF16),
        ),
        in_specs=[vmem(), anywhere()],
        name="slots",
        flops=10**8,
        limit=12,
    )
    w_far = pltpu.with_memory_space_constraint(w_out, pltpu.HBM)
    w_near = call(
        stage_kernel,
        (w_far, slot_cols),
        jax.ShapeDtypeStruct((feat, width // 2), BF16),
        in_specs=[pl.BlockSpec(memory_space=pltpu.HBM), anywhere()],
        scratch_shapes=[pltpu.SemaphoreType.DMA((8,))],
        name="stage",
        flops=10**8,
        limit=4,
    )
    group_total = call(
        total_kernel,
        (shared, w_near),
        jax.ShapeDtypeStruct(slice_shape, BF16),
        in_specs=[vmem(), anywhere()],
        name="total",
        limit=4,
    )
    earlier = [
        lax.ppermute(group_total, "seq", [(i, i + near * k) for i in range(n_seq - near * k)])
        for k in range(1, far)
    ]
    scanned = call(
        scan_kernel,
        (shared, *earlier),
        jax.ShapeDtypeStruct((near, *slice_shape), BF16),
        name="scan",
        limit=4,
    )
    prefix = lax.all_to_all(
        scanned.reshape(feat, HEAD_DIM),
        "seq",
        split_axis=0,
        concat_axis=0,
        tiled=True,
        axis_index_groups=groups,
    )
    inner = call(
        inner_kernel,
        (query, keys, values, states),
        jax.ShapeDtypeStruct((length, 2 * feat), F32),
        in_specs=[vmem()] * 3 + [anywhere()],
        name="inner",
        flops=4 * length * length * feat,
        limit=12,
    )
    partial_out = call(
        project_kernel,
        (inner, prefix, attn_gain.reshape(1, feat), w_near, w_far),
        pltpu.HBM((n_head, tok_rows, width), BF16),
        in_specs=[vmem()] * 4 + [pl.BlockSpec(memory_space=pltpu.HBM)],
        out_specs=pl.BlockSpec(memory_space=pltpu.HBM),
        scratch_shapes=[
            pltpu.VMEM((QUARTERS // 2, feat, part), BF16),
            pltpu.VMEM((length, feat), BF16),
            pltpu.VMEM((QUARTERS, n_head, tok_rows, part), BF16),
            pltpu.SemaphoreType.DMA((QUARTERS // 2,)),
            pltpu.SemaphoreType.DMA((QUARTERS,)),
        ],
        name="project",
        limit=12,
        flops=2 * length * feat * width,
    )
    summed = lax.all_to_all(partial_out, "head", split_axis=0, concat_axis=0, tiled=False)

    resid, sent = call(
        dispatch_kernel,
        (summed.reshape(n_head, tok_rows, width), tokens, moe_gain.reshape(1, width), pick),
        (
            pltpu.HBM((tok_rows, width), F32),
            jax.ShapeDtypeStruct((experts * piece, part), BF16),
        ),
        out_specs=(pl.BlockSpec(memory_space=pltpu.HBM), vmem()),
        scratch_shapes=[pltpu.VMEM((tok_rows, width), F32), pltpu.SemaphoreType.DMA],
        name="dispatch",
        limit=16,
        flops=2 * experts * piece * QUARTERS * tok_rows * part,
    )
    received = lax.all_to_all(sent, ("exp", "head"), split_axis=0, concat_axis=0, tiled=True)
    made = call(
        expert_kernel,
        (received, w_gate, w_up, w_down),
        jax.ShapeDtypeStruct((experts * piece, part), BF16),
        scratch_shapes=[
            pltpu.VMEM((experts * CAP, width), BF16),
            pltpu.VMEM((experts * piece, part), BF16),
            pltpu.VMEM((experts * piece, part), BF16),
            pltpu.SemaphoreType.DMA((experts // GROUP,)),
        ],
        out_specs=pl.BlockSpec(memory_space=pltpu.HBM),
        name="experts",
        limit=20,
        flops=6 * experts * CAP * width * w_gate.shape[1],
    )
    returned = lax.all_to_all(made, ("exp", "head"), split_axis=0, concat_axis=0, tiled=True)
    mixed = call(
        combine_kernel,
        (returned, resid, slot_cols, gates),
        jax.ShapeDtypeStruct((tok_rows, width), BF16),
        in_specs=[vmem(), pl.BlockSpec(memory_space=pltpu.HBM), vmem(), vmem()],
        scratch_shapes=[
            pltpu.VMEM((experts * CAP, width), BF16),
            pltpu.VMEM((tok_rows, width), F32),
            pltpu.SemaphoreType.DMA,
        ],
        name="combine",
        limit=16,
        flops=10**9,
    )
    return mixed[None]


def solution(mesh):
    in_specs = (
        P("exp", "seq", "head"),
        P("exp", "seq", "head"),
        P("exp", "seq", "head"),
        P("head"),
        P("head", None),
        P("exp", ("seq", "head"), None),
        P("exp", ("seq", "head"), None),
        P("exp", ("seq", "head"), None),
        P(),
        P(("exp", "head"), None, None),
        P(("exp", "head"), None, None),
        P(("exp", "head"), None, None),
    )
    out_specs = P("exp", ("seq", "head"), None)
    return jax.shard_map(
        on_device, mesh=mesh, in_specs=in_specs, out_specs=out_specs, check_vma=False
    )
```

```python
import functools
import math

import jax
import jax.numpy as jnp
from jax import lax
from jax.experimental import pallas as pl
from jax.experimental.pallas import tpu as pltpu
from jax.sharding import PartitionSpec as P

HEAD_DIM = 128
TOPK = 2
CAP = 6
QUARTERS = 4
GROUP = 8
EPSILON = 1e-06


BF16 = jnp.bfloat16
F32 = jnp.float32
I32 = jnp.int32


def vmem():
    return pl.BlockSpec(memory_space=pltpu.VMEM)


def call(kernel, args, out_shape, *, name, flops=10**6, limit=24, in_specs=None, **kwargs):
    outs = out_shape if isinstance(out_shape, tuple) else (out_shape,)
    if "out_specs" not in kwargs:
        kwargs["out_specs"] = tuple(vmem() for _ in outs) if isinstance(out_shape, tuple) else vmem()
    moved = sum(math.prod(a.shape) * jnp.dtype(a.dtype).itemsize for a in (*args, *outs))
    return pl.pallas_call(
        kernel,
        out_shape=out_shape,
        in_specs=in_specs or [vmem()] * len(args),
        cost_estimate=pl.CostEstimate(flops=flops, bytes_accessed=moved, transcendentals=0),
        compiler_params=pltpu.CompilerParams(vmem_limit_bytes=limit * 2**20),
        name=name,
        **kwargs,
    )(*args)


def anywhere():
    return pl.BlockSpec(memory_space=pl.ANY)


def dot(a, b, dims=((1,), (0,))):
    return lax.dot_general(a, b, (dims, ((), ())), preferred_element_type=F32)


def states_kernel(keys_hbm, values_hbm, out_ref, keys_ref, values_ref, sems):
    length, feat = keys_ref.shape
    chunks = sems.shape[1]
    rows = length // chunks
    copies = []
    for c in range(chunks):
        part = slice(c * rows, (c + 1) * rows)
        for k, (hbm, ref) in enumerate(((keys_hbm, keys_ref), (values_hbm, values_ref))):
            copies.append(pltpu.make_async_copy(hbm.at[part], ref.at[part], sems.at[k, c]))
            copies[-1].start()
    for copy in copies:
        copy.wait()
    for h in range(feat // HEAD_DIM):
        cols = slice(h * HEAD_DIM, (h + 1) * HEAD_DIM)
        state = dot(keys_ref[:, cols], values_ref[:, cols], ((0,), (0,)))
        out_ref[cols, :] = state.astype(out_ref.dtype)


def total_kernel(in_ref, after_ref, out_ref):
    total = in_ref[0].astype(F32)
    for b in range(1, in_ref.shape[0]):
        total = total + in_ref[b].astype(F32)
    out_ref[...] = total.astype(out_ref.dtype)


def scan_kernel(in_ref, *refs):
    *far_refs, out_ref = refs
    total = jnp.zeros(in_ref.shape[1:], F32)
    for far_ref in far_refs:
        total = total + far_ref[...].astype(F32)
    for b in range(in_ref.shape[0]):
        out_ref[b] = total.astype(out_ref.dtype)
        total = total + in_ref[b].astype(F32)


def slots_kernel(routes_ref, after_ref, cols_ref, pick_ref, *, experts):
    rows = routes_ref.shape[0]
    first, second = routes_ref[:, 0:1], routes_ref[:, 1:2]
    ids = lax.broadcasted_iota(I32, (rows, experts), 1)
    hit0 = (first == ids).astype(F32)
    hit1 = (second == ids).astype(F32)
    above = lax.broadcasted_iota(I32, (rows, rows), 0) > lax.broadcasted_iota(I32, (rows, rows), 1)
    before = dot(above.astype(F32).astype(BF16), (hit0 + hit1).astype(BF16))
    pos0 = jnp.sum(before * hit0, axis=1, keepdims=True)
    pos1 = jnp.sum(before * hit1, axis=1, keepdims=True)
    slot0 = first.astype(F32) * CAP + pos0
    slot1 = second.astype(F32) * CAP + pos1
    lane = lax.broadcasted_iota(I32, (rows, 128), 1)
    both = jnp.where(lane == 0, slot0, jnp.where(lane == 1, slot1, 0.0))
    cols_ref[...] = both.astype(I32)
    slots = both.T.astype(I32)
    key0 = jnp.concatenate([slots[0:1] * QUARTERS + q for q in range(QUARTERS)], axis=1)
    key1 = jnp.concatenate([slots[1:2] * QUARTERS + q for q in range(QUARTERS)], axis=1)
    total = pick_ref.shape[0]
    chunk = total // 4
    for b in range(4):
        keys = row_keys(chunk, b * chunk)
        pick = ((keys == key0) | (keys == key1)).astype(F32)
        pick_ref[b * chunk : (b + 1) * chunk, :] = pick.astype(BF16)


def inner_kernel(
    query_hbm, keys_hbm, values_hbm, after_ref, out_ref, query_ref, keys_ref, values_ref, sems
):
    heads, length, _ = keys_ref.shape
    feat = heads * HEAD_DIM
    loads = []
    for h in range(heads):
        cols = slice(h * HEAD_DIM, (h + 1) * HEAD_DIM)
        pairs = ((query_hbm, query_ref), (keys_hbm, keys_ref), (values_hbm, values_ref))
        for k, (hbm, ref) in enumerate(pairs):
            loads.append(pltpu.make_async_copy(hbm.at[:, cols], ref.at[h], sems.at[h, k]))
            loads[-1].start()
    rows = length // 4
    for h in range(heads):
        for load in loads[3 * h : 3 * h + 3]:
            load.wait()
        cols = slice(h * HEAD_DIM, (h + 1) * HEAD_DIM)
        out_ref[:, feat + h * HEAD_DIM : feat + (h + 1) * HEAD_DIM] = query_ref[h].astype(F32)
        for i in range(4):
            seen = (i + 1) * rows
            row_ids = lax.broadcasted_iota(I32, (rows, seen), 0) + i * rows
            causal = row_ids >= lax.broadcasted_iota(I32, (rows, seen), 1)
            q = query_ref[h, i * rows : (i + 1) * rows, :]
            scores = dot(q, keys_ref[h, 0:seen, :], ((1,), (1,)))
            scores = jnp.where(causal, scores, 0.0).astype(BF16)
            out_ref[i * rows : (i + 1) * rows, cols] = dot(scores, values_ref[h, 0:seen, :])


def stage_kernel(w_hbm, after_ref, w_ref, sems):
    pieces = sems.shape[0]
    rows = w_ref.shape[0] // pieces
    loads = []
    for p in range(pieces):
        part = slice(p * rows, (p + 1) * rows)
        source = w_hbm.at[part, 0 : w_ref.shape[1]]
        loads.append(pltpu.make_async_copy(source, w_ref.at[part], sems.at[p]))
        loads[-1].start()
    for load in loads:
        load.wait()


def project_kernel(
    inner_ref, prefix_ref, gain_ref, w_near_ref, w_hbm, out_ref, w_ref, normed_ref, part_ref, w_sems, sems
):
    steps, _, _, part = part_ref.shape
    ready = w_near_ref.shape[1] // part
    loads = []
    for j in range(ready, steps):
        source = w_hbm.at[:, j * part : (j + 1) * part]
        loads.append(pltpu.make_async_copy(source, w_ref.at[j - ready], w_sems.at[j - ready]))
        loads[-1].start()
    feat = normed_ref.shape[1]
    for h in range(feat // HEAD_DIM):
        cols = slice(h * HEAD_DIM, (h + 1) * HEAD_DIM)
        q = inner_ref[:, feat + h * HEAD_DIM : feat + (h + 1) * HEAD_DIM].astype(BF16)
        out = inner_ref[:, cols] + dot(q, prefix_ref[cols, :])
        scale = lax.rsqrt(jnp.mean(out * out, axis=-1, keepdims=True) + EPSILON)
        normed_ref[:, cols] = (out * scale * gain_ref[:, cols]).astype(BF16)
    copies = []
    for j in range(steps):
        cols = slice(j * part, (j + 1) * part)
        if j < ready:
            w = w_near_ref[:, cols]
        else:
            loads[j - ready].wait()
            w = w_ref[j - ready]
        part_ref[j] = dot(normed_ref[...], w).astype(BF16).reshape(part_ref.shape[1:])
        copies.append(pltpu.make_async_copy(part_ref.at[j], out_ref.at[:, :, cols], sems.at[j]))
        copies[-1].start()
    for copy in copies:
        copy.wait()


def row_keys(count, base):
    piece = QUARTERS * CAP
    r = lax.broadcasted_iota(I32, (count, 1), 0).astype(F32) + base
    e = jnp.floor((r + 0.5) * (1.0 / piece))
    rem = r - e * piece
    q = jnp.floor((rem + 0.5) * (1.0 / CAP))
    c = rem - q * CAP
    return (QUARTERS * (e * CAP + c) + q).astype(I32)


def dispatch_kernel(recv_ref, tokens_ref, gain_ref, pick_ref, resid_hbm, out_ref, resid_ref, sem):
    peers = recv_ref.shape[0]
    width = tokens_ref.shape[1]
    attn = recv_ref[0].astype(F32)
    for p in range(1, peers):
        attn = attn + recv_ref[p].astype(F32)
    resid = tokens_ref[...].astype(F32) + attn
    resid_ref[...] = resid
    copy = pltpu.make_async_copy(resid_ref, resid_hbm, sem)
    copy.start()
    scale = lax.rsqrt(jnp.mean(resid * resid, axis=-1, keepdims=True) + EPSILON)
    moe_in = (resid * scale * gain_ref[...]).astype(BF16)
    part = width // QUARTERS
    stacked = jnp.concatenate([moe_in[:, q * part : (q + 1) * part] for q in range(QUARTERS)], axis=0)
    out_ref[...] = dot(pick_ref[...], stacked).astype(BF16)
    copy.wait()


def regroup_matrix(to_pieces):
    n = GROUP * QUARTERS * CAP
    i = lax.broadcasted_iota(I32, (n, 1), 0).astype(F32)
    q = jnp.floor((i + 0.5) * (1.0 / (GROUP * CAP)))
    rem = i - q * (GROUP * CAP)
    p = jnp.floor((rem + 0.5) * (1.0 / CAP))
    c = rem - p * CAP
    source = (p * (QUARTERS * CAP) + q * CAP + c).astype(I32)
    j = lax.broadcasted_iota(I32, (n, n), 1)
    matrix = (source == j).astype(F32)
    if to_pieces:
        matrix = matrix.T
    return matrix.astype(BF16)


def expert_kernel(recv_ref, gate_ref, up_ref, down_ref, out_ref, x_ref, y_ref, z_ref, sems):
    rows, part = recv_ref.shape
    n = GROUP * QUARTERS * CAP
    m = n // QUARTERS
    gather = regroup_matrix(False)
    for g in range(rows // n):
        block = dot(gather, recv_ref[g * n : (g + 1) * n, :]).astype(BF16)
        for q in range(QUARTERS):
            x_ref[g * m : (g + 1) * m, q * part : (q + 1) * part] = block[q * m : (q + 1) * m, :]
    x = x_ref[...]
    gate = dot(x, gate_ref[...])
    up = dot(x, up_ref[...])
    hidden = (gate / (1.0 + jnp.exp(-gate)) * up).astype(BF16)
    for q in range(QUARTERS):
        made = dot(hidden, down_ref[:, q * part : (q + 1) * part]).astype(BF16)
        for g in range(rows // n):
            y_ref[g * n + q * m : g * n + (q + 1) * m, :] = made[g * m : (g + 1) * m, :]
    scatter = regroup_matrix(True)
    copies = []
    for g in range(rows // n):
        part_rows = slice(g * n, (g + 1) * n)
        z_ref[part_rows, :] = dot(scatter, y_ref[part_rows, :]).astype(BF16)
        copies.append(pltpu.make_async_copy(z_ref.at[part_rows], out_ref.at[part_rows], sems.at[g]))
        copies[-1].start()
    for copy in copies:
        copy.wait()


def combine_kernel(back_ref, resid_hbm, cols_ref, gates_ref, out_ref, y_ref, resid_ref, sem):
    rows, part = back_ref.shape
    tok_rows = resid_ref.shape[0]
    copy = pltpu.make_async_copy(resid_hbm, resid_ref, sem)
    copy.start()
    n = GROUP * QUARTERS * CAP
    m = n // QUARTERS
    gather = regroup_matrix(False)
    for g in range(rows // n):
        block = dot(gather, back_ref[g * n : (g + 1) * n, :]).astype(BF16)
        for q in range(QUARTERS):
            y_ref[g * m : (g + 1) * m, q * part : (q + 1) * part] = block[q * m : (q + 1) * m, :]
    y = y_ref[...]
    slot_total = y.shape[0]
    ids = lax.broadcasted_iota(I32, (tok_rows, slot_total), 1)
    moe = jnp.zeros(out_ref.shape, F32)
    for pick in range(TOPK):
        chosen = (cols_ref[:, pick : pick + 1] == ids).astype(F32).astype(BF16)
        moe = moe + gates_ref[:, pick : pick + 1] * dot(chosen, y)
    copy.wait()
    out_ref[...] = (resid_ref[...] + moe).astype(out_ref.dtype)


def on_device(
    query, keys, values, attn_gain, w_out, tokens, routes, gates, moe_gain, w_gate, w_up, w_down
):
    query, keys, values = query[0], keys[0], values[0]
    tokens, routes, gates = tokens[0], routes[0], gates[0]
    w_gate, w_up, w_down = w_gate[0], w_up[0], w_down[0]
    length, feat = query.shape
    tok_rows, width = tokens.shape
    n_seq, n_exp, n_head = (lax.axis_size(a) for a in ("seq", "exp", "head"))
    experts = n_exp * n_head
    part = width // QUARTERS
    piece = QUARTERS * CAP

    near = 4
    far = n_seq // near
    groups = [[near * g + i for i in range(near)] for g in range(far)]
    states = call(
        states_kernel,
        tuple(pltpu.with_memory_space_constraint(a, pltpu.HBM) for a in (keys, values)),
        jax.ShapeDtypeStruct((feat, HEAD_DIM), BF16),
        in_specs=[anywhere(), anywhere()],
        scratch_shapes=[
            pltpu.VMEM((length, feat), BF16),
            pltpu.VMEM((length, feat), BF16),
            pltpu.SemaphoreType.DMA((2, 4)),
        ],
        name="states",
        flops=2 * length * feat * HEAD_DIM,
        limit=8,
    )
    shared = lax.all_to_all(
        states, "seq", split_axis=0, concat_axis=0, tiled=True, axis_index_groups=groups
    ).reshape(near, feat // near, HEAD_DIM)
    slice_shape = (feat // near, HEAD_DIM)
    slot_cols, pick = call(
        functools.partial(slots_kernel, experts=experts),
        (routes, states),
        (
            jax.ShapeDtypeStruct((tok_rows, 128), I32),
            jax.ShapeDtypeStruct((experts * piece, QUARTERS * tok_rows), BF16),
        ),
        in_specs=[vmem(), anywhere()],
        name="slots",
        flops=10**8,
        limit=12,
    )
    group_total = call(
        total_kernel,
        (shared, slot_cols),
        jax.ShapeDtypeStruct(slice_shape, BF16),
        in_specs=[vmem(), anywhere()],
        name="total",
        limit=4,
    )
    earlier = [
        lax.ppermute(group_total, "seq", [(i, i + near * k) for i in range(n_seq - near * k)])
        for k in range(1, far)
    ]
    scanned = call(
        scan_kernel,
        (shared, *earlier),
        jax.ShapeDtypeStruct((near, *slice_shape), BF16),
        name="scan",
        limit=4,
    )
    w_far = pltpu.with_memory_space_constraint(w_out, pltpu.HBM)
    w_near = call(
        stage_kernel,
        (w_far, scanned),
        jax.ShapeDtypeStruct((feat, width // 2), BF16),
        in_specs=[pl.BlockSpec(memory_space=pltpu.HBM), anywhere()],
        scratch_shapes=[pltpu.SemaphoreType.DMA((8,))],
        name="stage",
        flops=10**8,
        limit=4,
    )
    prefix = lax.all_to_all(
        scanned.reshape(feat, HEAD_DIM),
        "seq",
        split_axis=0,
        concat_axis=0,
        tiled=True,
        axis_index_groups=groups,
    )
    heads = feat // HEAD_DIM
    inner = call(
        inner_kernel,
        (*(pltpu.with_memory_space_constraint(a, pltpu.HBM) for a in (query, keys, values)), scanned),
        jax.ShapeDtypeStruct((length, 2 * feat), F32),
        in_specs=[pl.BlockSpec(memory_space=pltpu.HBM)] * 3 + [anywhere()],
        scratch_shapes=[pltpu.VMEM((heads, length, HEAD_DIM), BF16)] * 3
        + [pltpu.SemaphoreType.DMA((heads, 3))],
        name="inner",
        flops=4 * length * length * feat,
        limit=12,
    )
    partial_out = call(
        project_kernel,
        (inner, prefix, attn_gain.reshape(1, feat), w_near, w_far),
        pltpu.HBM((n_head, tok_rows, width), BF16),
        in_specs=[vmem()] * 4 + [pl.BlockSpec(memory_space=pltpu.HBM)],
        out_specs=pl.BlockSpec(memory_space=pltpu.HBM),
        scratch_shapes=[
            pltpu.VMEM((QUARTERS // 2, feat, part), BF16),
            pltpu.VMEM((length, feat), BF16),
            pltpu.VMEM((QUARTERS, n_head, tok_rows, part), BF16),
            pltpu.SemaphoreType.DMA((QUARTERS // 2,)),
            pltpu.SemaphoreType.DMA((QUARTERS,)),
        ],
        name="project",
        limit=12,
        flops=2 * length * feat * width,
    )
    summed = lax.all_to_all(partial_out, "head", split_axis=0, concat_axis=0, tiled=False)

    resid, sent = call(
        dispatch_kernel,
        (summed.reshape(n_head, tok_rows, width), tokens, moe_gain.reshape(1, width), pick),
        (
            pltpu.HBM((tok_rows, width), F32),
            jax.ShapeDtypeStruct((experts * piece, part), BF16),
        ),
        out_specs=(pl.BlockSpec(memory_space=pltpu.HBM), vmem()),
        scratch_shapes=[pltpu.VMEM((tok_rows, width), F32), pltpu.SemaphoreType.DMA],
        name="dispatch",
        limit=16,
        flops=2 * experts * piece * QUARTERS * tok_rows * part,
    )
    received = lax.all_to_all(sent, ("exp", "head"), split_axis=0, concat_axis=0, tiled=True)
    made = call(
        expert_kernel,
        (received, w_gate, w_up, w_down),
        jax.ShapeDtypeStruct((experts * piece, part), BF16),
        scratch_shapes=[
            pltpu.VMEM((experts * CAP, width), BF16),
            pltpu.VMEM((experts * piece, part), BF16),
            pltpu.VMEM((experts * piece, part), BF16),
            pltpu.SemaphoreType.DMA((experts // GROUP,)),
        ],
        out_specs=pl.BlockSpec(memory_space=pltpu.HBM),
        name="experts",
        limit=20,
        flops=6 * experts * CAP * width * w_gate.shape[1],
    )
    returned = lax.all_to_all(made, ("exp", "head"), split_axis=0, concat_axis=0, tiled=True)
    mixed = call(
        combine_kernel,
        (returned, resid, slot_cols, gates),
        jax.ShapeDtypeStruct((tok_rows, width), BF16),
        in_specs=[vmem(), pl.BlockSpec(memory_space=pltpu.HBM), vmem(), vmem()],
        scratch_shapes=[
            pltpu.VMEM((experts * CAP, width), BF16),
            pltpu.VMEM((tok_rows, width), F32),
            pltpu.SemaphoreType.DMA,
        ],
        name="combine",
        limit=16,
        flops=10**9,
    )
    return mixed[None]


def solution(mesh):
    in_specs = (
        P("exp", "seq", "head"),
        P("exp", "seq", "head"),
        P("exp", "seq", "head"),
        P("head"),
        P("head", None),
        P("exp", ("seq", "head"), None),
        P("exp", ("seq", "head"), None),
        P("exp", ("seq", "head"), None),
        P(),
        P(("exp", "head"), None, None),
        P(("exp", "head"), None, None),
        P(("exp", "head"), None, None),
    )
    out_specs = P("exp", ("seq", "head"), None)
    return jax.shard_map(
        on_device, mesh=mesh, in_specs=in_specs, out_specs=out_specs, check_vma=False
    )
```

```python
import functools
import math

import jax
import jax.numpy as jnp
from jax import lax
from jax.experimental import pallas as pl
from jax.experimental.pallas import tpu as pltpu
from jax.sharding import PartitionSpec as P

HEAD_DIM = 128
TOPK = 2
CAP = 6
QUARTERS = 4
GROUP = 8
EPSILON = 1e-06


BF16 = jnp.bfloat16
F32 = jnp.float32
I32 = jnp.int32


def vmem():
    return pl.BlockSpec(memory_space=pltpu.VMEM)


def call(kernel, args, out_shape, *, name, flops=10**6, limit=24, in_specs=None, **kwargs):
    outs = out_shape if isinstance(out_shape, tuple) else (out_shape,)
    if "out_specs" not in kwargs:
        kwargs["out_specs"] = tuple(vmem() for _ in outs) if isinstance(out_shape, tuple) else vmem()
    moved = sum(math.prod(a.shape) * jnp.dtype(a.dtype).itemsize for a in (*args, *outs))
    return pl.pallas_call(
        kernel,
        out_shape=out_shape,
        in_specs=in_specs or [vmem()] * len(args),
        cost_estimate=pl.CostEstimate(flops=flops, bytes_accessed=moved, transcendentals=0),
        compiler_params=pltpu.CompilerParams(vmem_limit_bytes=limit * 2**20),
        name=name,
        **kwargs,
    )(*args)


def anywhere():
    return pl.BlockSpec(memory_space=pl.ANY)


def dot(a, b, dims=((1,), (0,))):
    return lax.dot_general(a, b, (dims, ((), ())), preferred_element_type=F32)


def states_kernel(keys_hbm, values_hbm, out_ref, keys_ref, values_ref, sems):
    length, feat = keys_ref.shape
    chunks = sems.shape[1]
    rows = length // chunks
    copies = []
    for c in range(chunks):
        part = slice(c * rows, (c + 1) * rows)
        for k, (hbm, ref) in enumerate(((keys_hbm, keys_ref), (values_hbm, values_ref))):
            copies.append(pltpu.make_async_copy(hbm.at[part], ref.at[part], sems.at[k, c]))
            copies[-1].start()
    for copy in copies:
        copy.wait()
    for h in range(feat // HEAD_DIM):
        cols = slice(h * HEAD_DIM, (h + 1) * HEAD_DIM)
        state = dot(keys_ref[:, cols], values_ref[:, cols], ((0,), (0,)))
        out_ref[cols, :] = state.astype(out_ref.dtype)


def total_kernel(in_ref, after_ref, out_ref):
    total = in_ref[0].astype(F32)
    for b in range(1, in_ref.shape[0]):
        total = total + in_ref[b].astype(F32)
    out_ref[...] = total.astype(out_ref.dtype)


def scan_kernel(in_ref, *refs):
    *far_refs, out_ref = refs
    total = jnp.zeros(in_ref.shape[1:], F32)
    for far_ref in far_refs:
        total = total + far_ref[...].astype(F32)
    for b in range(in_ref.shape[0]):
        out_ref[b] = total.astype(out_ref.dtype)
        total = total + in_ref[b].astype(F32)


def slots_kernel(routes_ref, after_ref, cols_ref, pick_ref, *, experts):
    rows = routes_ref.shape[0]
    first, second = routes_ref[:, 0:1], routes_ref[:, 1:2]
    ids = lax.broadcasted_iota(I32, (rows, experts), 1)
    hit0 = (first == ids).astype(F32)
    hit1 = (second == ids).astype(F32)
    above = lax.broadcasted_iota(I32, (rows, rows), 0) > lax.broadcasted_iota(I32, (rows, rows), 1)
    before = dot(above.astype(F32).astype(BF16), (hit0 + hit1).astype(BF16))
    pos0 = jnp.sum(before * hit0, axis=1, keepdims=True)
    pos1 = jnp.sum(before * hit1, axis=1, keepdims=True)
    slot0 = first.astype(F32) * CAP + pos0
    slot1 = second.astype(F32) * CAP + pos1
    lane = lax.broadcasted_iota(I32, (rows, 128), 1)
    both = jnp.where(lane == 0, slot0, jnp.where(lane == 1, slot1, 0.0))
    cols_ref[...] = both.astype(I32)
    slots = both.T.astype(I32)
    key0 = jnp.concatenate([slots[0:1] * QUARTERS + q for q in range(QUARTERS)], axis=1)
    key1 = jnp.concatenate([slots[1:2] * QUARTERS + q for q in range(QUARTERS)], axis=1)
    total = pick_ref.shape[0]
    chunk = total // 4
    for b in range(4):
        keys = lax.broadcasted_iota(I32, (chunk, 1), 0) + b * chunk
        pick = ((keys == key0) | (keys == key1)).astype(F32)
        pick_ref[b * chunk : (b + 1) * chunk, :] = pick.astype(BF16)


def inner_kernel(
    query_hbm, keys_hbm, values_hbm, after_ref, out_ref, query_ref, keys_ref, values_ref, sems
):
    heads, length, _ = keys_ref.shape
    feat = heads * HEAD_DIM
    loads = []
    for h in range(heads):
        cols = slice(h * HEAD_DIM, (h + 1) * HEAD_DIM)
        pairs = ((query_hbm, query_ref), (keys_hbm, keys_ref), (values_hbm, values_ref))
        for k, (hbm, ref) in enumerate(pairs):
            loads.append(pltpu.make_async_copy(hbm.at[:, cols], ref.at[h], sems.at[h, k]))
            loads[-1].start()
    rows = length // 4
    for h in range(heads):
        for load in loads[3 * h : 3 * h + 3]:
            load.wait()
        cols = slice(h * HEAD_DIM, (h + 1) * HEAD_DIM)
        out_ref[:, feat + h * HEAD_DIM : feat + (h + 1) * HEAD_DIM] = query_ref[h].astype(F32)
        for i in range(4):
            seen = (i + 1) * rows
            row_ids = lax.broadcasted_iota(I32, (rows, seen), 0) + i * rows
            causal = row_ids >= lax.broadcasted_iota(I32, (rows, seen), 1)
            q = query_ref[h, i * rows : (i + 1) * rows, :]
            scores = dot(q, keys_ref[h, 0:seen, :], ((1,), (1,)))
            scores = jnp.where(causal, scores, 0.0).astype(BF16)
            out_ref[i * rows : (i + 1) * rows, cols] = dot(scores, values_ref[h, 0:seen, :])


def stage_kernel(w_hbm, after_ref, w_ref, sems):
    pieces = sems.shape[0]
    rows = w_ref.shape[0] // pieces
    loads = []
    for p in range(pieces):
        part = slice(p * rows, (p + 1) * rows)
        source = w_hbm.at[part, 0 : w_ref.shape[1]]
        loads.append(pltpu.make_async_copy(source, w_ref.at[part], sems.at[p]))
        loads[-1].start()
    for load in loads:
        load.wait()


def project_kernel(
    inner_ref, prefix_ref, gain_ref, w_near_ref, w_hbm, out_ref, w_ref, normed_ref, part_ref, w_sems, sems
):
    steps, _, _, part = part_ref.shape
    ready = w_near_ref.shape[1] // part
    loads = []
    for j in range(ready, steps):
        source = w_hbm.at[:, j * part : (j + 1) * part]
        loads.append(pltpu.make_async_copy(source, w_ref.at[j - ready], w_sems.at[j - ready]))
        loads[-1].start()
    feat = normed_ref.shape[1]
    for h in range(feat // HEAD_DIM):
        cols = slice(h * HEAD_DIM, (h + 1) * HEAD_DIM)
        q = inner_ref[:, feat + h * HEAD_DIM : feat + (h + 1) * HEAD_DIM].astype(BF16)
        out = inner_ref[:, cols] + dot(q, prefix_ref[cols, :])
        scale = lax.rsqrt(jnp.mean(out * out, axis=-1, keepdims=True) + EPSILON)
        normed_ref[:, cols] = (out * scale * gain_ref[:, cols]).astype(BF16)
    copies = []
    for j in range(steps):
        cols = slice(j * part, (j + 1) * part)
        if j < ready:
            w = w_near_ref[:, cols]
        else:
            loads[j - ready].wait()
            w = w_ref[j - ready]
        part_ref[j] = dot(normed_ref[...], w).astype(BF16).reshape(part_ref.shape[1:])
        copies.append(pltpu.make_async_copy(part_ref.at[j], out_ref.at[:, :, cols], sems.at[j]))
        copies[-1].start()
    for copy in copies:
        copy.wait()


def dispatch_kernel(recv_ref, tokens_ref, gain_ref, pick_ref, resid_hbm, out_ref, resid_ref, sem):
    peers = recv_ref.shape[0]
    width = tokens_ref.shape[1]
    attn = recv_ref[0].astype(F32)
    for p in range(1, peers):
        attn = attn + recv_ref[p].astype(F32)
    resid = tokens_ref[...].astype(F32) + attn
    resid_ref[...] = resid
    copy = pltpu.make_async_copy(resid_ref, resid_hbm, sem)
    copy.start()
    scale = lax.rsqrt(jnp.mean(resid * resid, axis=-1, keepdims=True) + EPSILON)
    moe_in = (resid * scale * gain_ref[...]).astype(BF16)
    part = width // QUARTERS
    stacked = jnp.concatenate([moe_in[:, q * part : (q + 1) * part] for q in range(QUARTERS)], axis=0)
    out_ref[...] = dot(pick_ref[...], stacked).astype(BF16)
    copy.wait()


def split_quarters(pieces_ref, wide_ref, out_ref):
    rows, part = pieces_ref.shape
    slots = rows // QUARTERS
    lanes = part // 128
    for l in range(lanes):
        wide_ref[l] = pieces_ref[:, l * 128 : (l + 1) * 128].astype(F32)
    for q in range(QUARTERS):
        for l in range(lanes):
            cols = slice(q * part + l * 128, q * part + (l + 1) * 128)
            block = wide_ref[l, pl.ds(q, slots, stride=QUARTERS), :]
            out_ref[:, cols] = block.astype(BF16)


def expert_kernel(recv_ref, gate_ref, up_ref, down_ref, out_ref, x_ref, wide_ref, z_ref, sems):
    rows, part = recv_ref.shape
    slots = rows // QUARTERS
    lanes = part // 128
    split_quarters(recv_ref, wide_ref, x_ref)
    x = x_ref[...]
    gate = dot(x, gate_ref[...])
    up = dot(x, up_ref[...])
    hidden = (gate / (1.0 + jnp.exp(-gate)) * up).astype(BF16)
    for q in range(QUARTERS):
        made = dot(hidden, down_ref[:, q * part : (q + 1) * part])
        for l in range(lanes):
            wide_ref[l, pl.ds(q, slots, stride=QUARTERS), :] = made[:, l * 128 : (l + 1) * 128]
    copies = []
    pieces = sems.shape[0]
    n = rows // pieces
    for g in range(pieces):
        part_rows = slice(g * n, (g + 1) * n)
        for l in range(lanes):
            z_ref[part_rows, l * 128 : (l + 1) * 128] = wide_ref[l, part_rows, :].astype(BF16)
        copies.append(pltpu.make_async_copy(z_ref.at[part_rows], out_ref.at[part_rows], sems.at[g]))
        copies[-1].start()
    for copy in copies:
        copy.wait()


def combine_kernel(
    back_ref, resid_hbm, cols_ref, gates_ref, out_ref, y_ref, wide_ref, resid_ref, sem
):
    tok_rows = resid_ref.shape[0]
    copy = pltpu.make_async_copy(resid_hbm, resid_ref, sem)
    copy.start()
    split_quarters(back_ref, wide_ref, y_ref)
    y = y_ref[...]
    slot_total = y.shape[0]
    ids = lax.broadcasted_iota(I32, (tok_rows, slot_total), 1)
    moe = jnp.zeros(out_ref.shape, F32)
    for pick in range(TOPK):
        chosen = (cols_ref[:, pick : pick + 1] == ids).astype(F32).astype(BF16)
        moe = moe + gates_ref[:, pick : pick + 1] * dot(chosen, y)
    copy.wait()
    out_ref[...] = (resid_ref[...] + moe).astype(out_ref.dtype)


def on_device(
    query, keys, values, attn_gain, w_out, tokens, routes, gates, moe_gain, w_gate, w_up, w_down
):
    query, keys, values = query[0], keys[0], values[0]
    tokens, routes, gates = tokens[0], routes[0], gates[0]
    w_gate, w_up, w_down = w_gate[0], w_up[0], w_down[0]
    length, feat = query.shape
    tok_rows, width = tokens.shape
    n_seq, n_exp, n_head = (lax.axis_size(a) for a in ("seq", "exp", "head"))
    experts = n_exp * n_head
    part = width // QUARTERS
    piece = QUARTERS * CAP

    near = 4
    far = n_seq // near
    groups = [[near * g + i for i in range(near)] for g in range(far)]
    states = call(
        states_kernel,
        tuple(pltpu.with_memory_space_constraint(a, pltpu.HBM) for a in (keys, values)),
        jax.ShapeDtypeStruct((feat, HEAD_DIM), BF16),
        in_specs=[anywhere(), anywhere()],
        scratch_shapes=[
            pltpu.VMEM((length, feat), BF16),
            pltpu.VMEM((length, feat), BF16),
            pltpu.SemaphoreType.DMA((2, 4)),
        ],
        name="states",
        flops=2 * length * feat * HEAD_DIM,
        limit=8,
    )
    shared = lax.all_to_all(
        states, "seq", split_axis=0, concat_axis=0, tiled=True, axis_index_groups=groups
    ).reshape(near, feat // near, HEAD_DIM)
    slice_shape = (feat // near, HEAD_DIM)
    slot_cols, pick = call(
        functools.partial(slots_kernel, experts=experts),
        (routes, states),
        (
            jax.ShapeDtypeStruct((tok_rows, 128), I32),
            jax.ShapeDtypeStruct((experts * piece, QUARTERS * tok_rows), BF16),
        ),
        in_specs=[vmem(), anywhere()],
        name="slots",
        flops=10**8,
        limit=12,
    )
    group_total = call(
        total_kernel,
        (shared, slot_cols),
        jax.ShapeDtypeStruct(slice_shape, BF16),
        in_specs=[vmem(), anywhere()],
        name="total",
        limit=4,
    )
    earlier = [
        lax.ppermute(group_total, "seq", [(i, i + near * k) for i in range(n_seq - near * k)])
        for k in range(1, far)
    ]
    scanned = call(
        scan_kernel,
        (shared, *earlier),
        jax.ShapeDtypeStruct((near, *slice_shape), BF16),
        name="scan",
        limit=4,
    )
    w_far = pltpu.with_memory_space_constraint(w_out, pltpu.HBM)
    w_near = call(
        stage_kernel,
        (w_far, scanned),
        jax.ShapeDtypeStruct((feat, width // 2), BF16),
        in_specs=[pl.BlockSpec(memory_space=pltpu.HBM), anywhere()],
        scratch_shapes=[pltpu.SemaphoreType.DMA((8,))],
        name="stage",
        flops=10**8,
        limit=4,
    )
    prefix = lax.all_to_all(
        scanned.reshape(feat, HEAD_DIM),
        "seq",
        split_axis=0,
        concat_axis=0,
        tiled=True,
        axis_index_groups=groups,
    )
    heads = feat // HEAD_DIM
    inner = call(
        inner_kernel,
        (*(pltpu.with_memory_space_constraint(a, pltpu.HBM) for a in (query, keys, values)), scanned),
        jax.ShapeDtypeStruct((length, 2 * feat), F32),
        in_specs=[pl.BlockSpec(memory_space=pltpu.HBM)] * 3 + [anywhere()],
        scratch_shapes=[pltpu.VMEM((heads, length, HEAD_DIM), BF16)] * 3
        + [pltpu.SemaphoreType.DMA((heads, 3))],
        name="inner",
        flops=4 * length * length * feat,
        limit=12,
    )
    partial_out = call(
        project_kernel,
        (inner, prefix, attn_gain.reshape(1, feat), w_near, w_far),
        pltpu.HBM((n_head, tok_rows, width), BF16),
        in_specs=[vmem()] * 4 + [pl.BlockSpec(memory_space=pltpu.HBM)],
        out_specs=pl.BlockSpec(memory_space=pltpu.HBM),
        scratch_shapes=[
            pltpu.VMEM((QUARTERS // 2, feat, part), BF16),
            pltpu.VMEM((length, feat), BF16),
            pltpu.VMEM((QUARTERS, n_head, tok_rows, part), BF16),
            pltpu.SemaphoreType.DMA((QUARTERS // 2,)),
            pltpu.SemaphoreType.DMA((QUARTERS,)),
        ],
        name="project",
        limit=12,
        flops=2 * length * feat * width,
    )
    summed = lax.all_to_all(partial_out, "head", split_axis=0, concat_axis=0, tiled=False)

    resid, sent = call(
        dispatch_kernel,
        (summed.reshape(n_head, tok_rows, width), tokens, moe_gain.reshape(1, width), pick),
        (
            pltpu.HBM((tok_rows, width), F32),
            jax.ShapeDtypeStruct((experts * piece, part), BF16),
        ),
        out_specs=(pl.BlockSpec(memory_space=pltpu.HBM), vmem()),
        scratch_shapes=[pltpu.VMEM((tok_rows, width), F32), pltpu.SemaphoreType.DMA],
        name="dispatch",
        limit=16,
        flops=2 * experts * piece * QUARTERS * tok_rows * part,
    )
    received = lax.all_to_all(sent, ("exp", "head"), split_axis=0, concat_axis=0, tiled=True)
    made = call(
        expert_kernel,
        (received, w_gate, w_up, w_down),
        jax.ShapeDtypeStruct((experts * piece, part), BF16),
        scratch_shapes=[
            pltpu.VMEM((experts * CAP, width), BF16),
            pltpu.VMEM((part // 128, experts * piece, 128), F32),
            pltpu.VMEM((experts * piece, part), BF16),
            pltpu.SemaphoreType.DMA((experts // GROUP,)),
        ],
        out_specs=pl.BlockSpec(memory_space=pltpu.HBM),
        name="experts",
        limit=20,
        flops=6 * experts * CAP * width * w_gate.shape[1],
    )
    returned = lax.all_to_all(made, ("exp", "head"), split_axis=0, concat_axis=0, tiled=True)
    mixed = call(
        combine_kernel,
        (returned, resid, slot_cols, gates),
        jax.ShapeDtypeStruct((tok_rows, width), BF16),
        in_specs=[vmem(), pl.BlockSpec(memory_space=pltpu.HBM), vmem(), vmem()],
        scratch_shapes=[
            pltpu.VMEM((experts * CAP, width), BF16),
            pltpu.VMEM((part // 128, experts * piece, 128), F32),
            pltpu.VMEM((tok_rows, width), F32),
            pltpu.SemaphoreType.DMA,
        ],
        name="combine",
        limit=16,
        flops=10**9,
    )
    return mixed[None]


def solution(mesh):
    in_specs = (
        P("exp", "seq", "head"),
        P("exp", "seq", "head"),
        P("exp", "seq", "head"),
        P("head"),
        P("head", None),
        P("exp", ("seq", "head"), None),
        P("exp", ("seq", "head"), None),
        P("exp", ("seq", "head"), None),
        P(),
        P(("exp", "head"), None, None),
        P(("exp", "head"), None, None),
        P(("exp", "head"), None, None),
    )
    out_specs = P("exp", ("seq", "head"), None)
    return jax.shard_map(
        on_device, mesh=mesh, in_specs=in_specs, out_specs=out_specs, check_vma=False
    )
```
